32 devices in a mesh: scene: 2 (over x), slab: 4 (over y, core), sub: 4 (over z).
Axes of the slice: x: 2, y: 2, z: 4, core: 2. Of those that a mesh axis runs over, the one named last changes fastest.
Arguments:
- coarse_in: bfloat16 [32, 128, 16, 128], P(('scene', 'slab'), 'sub'), parts along dimension 0, may hold values from -110 to 290
- coarse_weight: bfloat16 [27, 128, 128], replicated, may hold values from -0.109375 to 0.109375
- norm_gain: float32 [128], replicated, may hold values from 0.25 to 1.75
- norm_bias: float32 [128], replicated, may hold values from -3 to 3
- lift_weight: bfloat16 [128, 128], replicated, may hold values from -0.5 to 0.5
- fine_input: bfloat16 [256, 512, 128], P(('scene', 'slab', 'sub')), parts along dimension 0, may hold values from -6 to 6
- block_coords: int32 [256, 3], P(('scene', 'slab', 'sub')), parts along dimension 0, may hold values from 0 to 31, as said below
- neighbours: int32 [256, 6], P(('scene', 'slab', 'sub')), parts along dimension 0, may hold values from -1 to 127, as said below
- fine_weight: bfloat16 [27, 128, 128], replicated, may hold values from -0.109375 to 0.109375
Outputs:
- fine_out: bfloat16 [256, 512, 128], P(('scene', 'slab', 'sub')), parts along dimension 0
The draws below stay inside these ranges and needn't reach their ends.
There are 2 independent parts, one for each index of `scene`. The reference program is written for one: setup_inputs(seed, part) draws one part's arguments, and reference() takes and returns one part's arrays. A program takes and returns all parts, laid end to end along the dimension named above; an argument that names none is the same for every part. Nothing has to cross between parts.
Inputs may be any that keep to these rules, and one draw needn't show every extreme that they name: `block_coords`: rows name distinct blocks. The 8 blocks of one device form 8 // 4 clusters of 2 x 2 x 1 face-adjacent blocks (first and second coordinate), each with its first coordinate in an aligned pair (2 p, 2 p + 1) and no two clusters of a device in the same pair, so that exactly 0 or 2 of one device's blocks have any given first coordinate. Every block of the device with sub index u has its second coordinate in [u * 8, (u + 1) * 8). Within a device the blocks stand in any order. `neighbours`: entries are row indices of all blocks of the scene. Entry d names the listed block that shares a face with the row's block on side d, in the order -first, +first, -second, +second, -third, +third coordinate, or is -1. Each block lists exactly two, both of its own cluster, so every listed block belongs to the same device; the lists are symmetric.
All inputs are finite; a program needn't handle non-finite values.
Results may differ from the reference program's by a relative error of at most 0.0056.
Values may be sent and summed in bfloat16 or wider, within the bound.
No kernel may reach another device: no remote copies, remote signals or barrier semaphores. Data moves between devices by JAX's collectives and lax.ppermute only.
A program may use at most 128 MiB of HBM per device.

```python
import jax
import jax.numpy as jnp
import numpy as np
from jax import lax

C = 128
G = 32
FB = 8
CY = 32
CZ = 16
BLK_DEV = 8
NX = 16
NY = 128
NZ = 16
NB = 128
N_SLAB = 4
N_SUB = 4


def link_table(member_total):
    table = np.full((member_total, 6), -1, dtype=np.int32)
    for member in range(member_total):
        within = member % 4
        for which_axis, stride in ((0, 2), (1, 1)):
            if within // stride % 2 == 1:
                table[member, 2 * which_axis] = member - stride
            else:
                table[member, 2 * which_axis + 1] = member + stride
    return table


def block_layout(key):
    base_key = jax.random.fold_in(key, 7)
    cube_edge = FB // 2
    x_pairs = N_SLAB // 2
    y_blocks = CY // cube_edge
    y_pairs = y_blocks // 2
    z_blocks = CZ // cube_edge
    slot_total = y_pairs * z_blocks
    clusters = BLK_DEV // 4
    pair_keys = jax.random.split(jax.random.fold_in(base_key, 1), N_SUB * x_pairs)
    chosen = jax.vmap(lambda single: jax.random.permutation(single, slot_total)[:2 * clusters])(pair_keys)
    chosen = chosen.reshape(N_SUB, x_pairs, 2 * clusters)
    column_keys = jax.random.split(jax.random.fold_in(base_key, 2), N_SUB)
    ticket = jax.vmap(lambda single: jax.random.permutation(single, N_SLAB))(column_keys)
    column = jnp.arange(N_SUB, dtype=jnp.int32)[:, None]
    cluster_list = []
    for which in range(clusters):
        pair_index = (ticket // 2 + which) % x_pairs
        slot_index = chosen[column, pair_index, 2 * which + ticket % 2]
        anchor_x = 2 * pair_index
        anchor_y = column * y_blocks + 2 * (slot_index // z_blocks)
        anchor_z = slot_index % z_blocks
        cluster_list.append(jnp.stack([anchor_x, anchor_y, anchor_z], axis=-1))
    anchors = jnp.stack(cluster_list, axis=2)
    anchors = anchors.transpose(1, 0, 2, 3)
    members = jnp.arange(4, dtype=jnp.int32)
    offsets = jnp.stack([members // 2, members % 2, members * 0], axis=-1)
    raw_coords = anchors[:, :, :, None, :] + offsets[None, None, None]
    raw_coords = raw_coords.reshape(N_SLAB, N_SUB, BLK_DEV, 3)
    order_keys = jax.random.split(jax.random.fold_in(base_key, 4), N_SLAB * N_SUB)
    block_order = jax.vmap(lambda single: jax.random.permutation(single, BLK_DEV))(order_keys)
    block_order = block_order.reshape(N_SLAB, N_SUB, BLK_DEV).astype(jnp.int32)
    inverse = jnp.argsort(block_order, axis=2, stable=True).astype(jnp.int32)
    coordinates = jnp.take_along_axis(raw_coords, block_order[..., None], axis=2)
    table = jnp.asarray(link_table(BLK_DEV))
    linked = table[block_order]
    valid = linked >= 0
    positions = jnp.take_along_axis(inverse, jnp.maximum(linked, 0).reshape(N_SLAB, N_SUB, BLK_DEV * 6), axis=2)
    positions = positions.reshape(N_SLAB, N_SUB, BLK_DEV, 6)
    device = jnp.arange(N_SLAB, dtype=jnp.int32)[:, None] * N_SUB + jnp.arange(N_SUB, dtype=jnp.int32)[None, :]
    global_ids = device[:, :, None, None] * BLK_DEV + positions
    global_ids = jnp.where(valid, global_ids, -1)
    return (coordinates.reshape(NB, 3).astype(jnp.int32), global_ids.reshape(NB, 6).astype(jnp.int32))


def draw_block_coords(key, part):
    return block_layout(key)[0]


def draw_neighbours(key, part):
    return block_layout(key)[1]


def draw_coarse_in(key, part):
    base_key = jax.random.fold_in(key, 11)
    key_list = jax.random.split(base_key, 2)
    position = jnp.arange(NX, dtype=jnp.float32) / (NX - 1)
    chan_mean = jax.random.uniform(key_list[0], (C,), jnp.float32, 0.5, 1.5)
    noise_field = jnp.clip(jax.random.normal(key_list[1], (NX, NY, NZ, C), jnp.float32), -4.0, 4.0)
    ramp_x = 1.0 + 2.0 * position
    scales = ramp_x[:, None, None, None]
    return (scales * (noise_field + chan_mean)).astype(jnp.bfloat16)


def block_scale(rng, dims, cuts, low, largest):
    level = 1.0
    for dim, shards_of in cuts:
        heights = jax.random.uniform(jax.random.fold_in(jax.random.fold_in(rng, 6), dim), (shards_of,), jnp.float32, low / len(cuts), largest / len(cuts))
        level = level * jnp.repeat(jnp.exp(heights), dims[dim] // shards_of).reshape((-1,) + (1,) * (len(dims) - 1 - dim))
    return level


def normal_values(key, extent, scale, bound, cuts=(), kind=jnp.bfloat16):
    drawn = scale * jax.random.normal(key, extent, jnp.float32)
    if cuts:
        drawn = drawn * block_scale(key, extent, cuts, -0.22, 0.18)
    return jnp.clip(drawn, -bound, bound).astype(kind)


def setup_inputs(seed: int = 0, part: int = 0) -> dict:
    key_of = jax.random.split(jax.random.key(seed), 10)
    part_splits = jax.random.split(jax.random.fold_in(key_of[9], part), 10)
    coarse_in = draw_coarse_in(jax.random.fold_in(jax.random.fold_in(key_of[9], part), 71), part)
    coarse_weight = normal_values(key_of[1], (27, C, C), (27 * C) ** -0.5, 0.109375)
    norm_gain = jnp.clip(1.0 + 0.15 * jax.random.normal(key_of[2], (C,), jnp.float32), 0.25, 1.75)
    norm_bias = normal_values(key_of[3], (C,), 0.5, 3.0, (), jnp.float32)
    lift_weight = normal_values(key_of[4], (C, C), C ** -0.5, 0.5)
    fine_input = normal_values(part_splits[5], (NB, FB**3, C), 1.0, 6.0, ((0, 16),))
    block_coords = draw_block_coords(jax.random.fold_in(jax.random.fold_in(key_of[9], part), 71), part)
    neighbours = draw_neighbours(jax.random.fold_in(jax.random.fold_in(key_of[9], part), 71), part)
    fine_weight = normal_values(key_of[8], (27, C, C), (27 * C) ** -0.5, 0.109375)
    return dict(coarse_in=coarse_in, coarse_weight=coarse_weight, norm_gain=norm_gain, norm_bias=norm_bias, lift_weight=lift_weight, fine_input=fine_input, block_coords=block_coords, neighbours=neighbours, fine_weight=fine_weight)


def convolve(padded, weights):
    batches = padded.shape[0]
    span_x = padded.shape[1] - 2
    span_y = padded.shape[2] - 2
    span_z = padded.shape[3] - 2
    channels = padded.shape[4]
    summed = jnp.zeros((batches * span_x * span_y * span_z, channels), jnp.float32)
    for along_x in range(3):
        for along_y in range(3):
            window = jnp.concatenate([padded[:, along_x:along_x + span_x, along_y:along_y + span_y, along_z:along_z + span_z, :] for along_z in range(3)], axis=-1)
            window = window.reshape(-1, 3 * channels)
            first_tap = 9 * along_x + 3 * along_y
            stacked = weights[first_tap:first_tap + 3].reshape(3 * channels, channels)
            summed = summed + jnp.dot(window, stacked, preferred_element_type=jnp.float32)
    return summed

def upsample(pieces):
    batches = pieces.shape[0]
    channels = pieces.shape[2]
    cube_edge = FB // 2
    stretched = pieces.reshape(batches, cube_edge, 1, cube_edge, 1, cube_edge, 1, channels)
    stretched = jnp.broadcast_to(stretched, (batches, cube_edge, 2, cube_edge, 2, cube_edge, 2, channels))
    return stretched.reshape(batches, FB * FB * FB, channels)

def block_planes(blocks):
    return (blocks[:, -1], blocks[:, 0], blocks[:, :, -1], blocks[:, :, 0], blocks[:, :, :, -1], blocks[:, :, :, 0])

def framed(blocks, planes, links):
    padded = jnp.pad(blocks, ((0, 0), (1, 1), (1, 1), (1, 1), (0, 0)))
    faces = []
    for direction in range(6):
        target = links[:, direction]
        picked = jnp.take(planes[direction], jnp.maximum(target, 0), axis=0)
        faces.append(jnp.where((target >= 0)[:, None, None, None], picked, jnp.zeros_like(picked)))
    padded = padded.at[:, 0, 1:-1, 1:-1].set(faces[0])
    padded = padded.at[:, -1, 1:-1, 1:-1].set(faces[1])
    padded = padded.at[:, 1:-1, 0, 1:-1].set(faces[2])
    padded = padded.at[:, 1:-1, -1, 1:-1].set(faces[3])
    padded = padded.at[:, 1:-1, 1:-1, 0].set(faces[4])
    padded = padded.at[:, 1:-1, 1:-1, -1].set(faces[5])
    return padded

def reference(coarse_in, coarse_weight, norm_gain, norm_bias, lift_weight, fine_input, block_coords, neighbours, fine_weight):
    padded = jnp.pad(coarse_in, ((1, 1), (1, 1), (1, 1), (0, 0)))[None]
    filtered = convolve(padded, coarse_weight).reshape(NX * NY * NZ, G, C // G)
    group_mean = lax.optimization_barrier(jnp.mean(filtered, axis=(0, 2)))
    centred = filtered - group_mean[None, :, None]
    spread = lax.optimization_barrier(jnp.mean(centred * centred, axis=(0, 2)))
    normed = centred * lax.rsqrt(spread + 1e-05)[None, :, None]
    normed = normed.reshape(-1, C) * norm_gain + norm_bias
    activated = jax.nn.silu(normed).astype(jnp.bfloat16)
    lifted = jnp.dot(activated, lift_weight, preferred_element_type=jnp.float32).astype(jnp.bfloat16)
    cube_edge = FB // 2
    cube_stock = lifted.reshape(NX // cube_edge, cube_edge, NY // cube_edge, cube_edge, NZ // cube_edge, cube_edge, C)
    cube_stock = cube_stock.transpose(0, 2, 4, 1, 3, 5, 6)
    chosen = cube_stock[block_coords[:, 0], block_coords[:, 1], block_coords[:, 2]]
    chosen = chosen.reshape(NB, cube_edge ** 3, C)
    block_input = (fine_input.astype(jnp.float32) + upsample(chosen).astype(jnp.float32)).astype(jnp.bfloat16)
    blocks = block_input.reshape(NB, FB, FB, FB, C)
    planes = block_planes(blocks)

    def one_group(group_index):
        first_row = group_index * BLK_DEV
        local_blocks = lax.dynamic_slice_in_dim(blocks, first_row, BLK_DEV, 0)
        local_links = lax.dynamic_slice_in_dim(neighbours, first_row, BLK_DEV, 0)
        summed = convolve(framed(local_blocks, planes, local_links), fine_weight)
        result = local_blocks.reshape(-1, C).astype(jnp.float32) + summed
        return result.astype(jnp.bfloat16).reshape(BLK_DEV, FB * FB * FB, C)
    outputs = lax.map(one_group, jnp.arange(NB // BLK_DEV, dtype=jnp.int32))
    return outputs.reshape(NB, FB * FB * FB, C)
```

```python
import functools

import jax
import jax.numpy as jnp
from jax import lax
from jax.experimental import pallas as pl
from jax.experimental.pallas import tpu as pltpu
from jax.sharding import PartitionSpec as P

G = 32
FB = 8
MOST = 2
EPS = 1e-05
F32 = jnp.float32
BF16 = jnp.bfloat16


def pairs(count, odd):
    links = []
    for i in range(odd, count - 1, 2):
        links += [(i, i + 1), (i + 1, i)]
    return links


def xor_links(count, distance):
    return [(i, i ^ distance) for i in range(count)]


def tap_sums(taken, weight_ref):
    window = jnp.concatenate(taken, axis=1)
    return jnp.dot(window, weight_ref, preferred_element_type=F32)


def shifted_sum(sums, depth, channels):
    rows = sums.shape[0]
    place = lax.broadcasted_iota(jnp.int32, (rows, channels), 0) % depth
    below = pltpu.roll(sums[:, :channels], 1, 0)
    above = pltpu.roll(sums[:, 2 * channels :], rows - 1, 0)
    return (
        sums[:, channels : 2 * channels]
        + jnp.where(place == 0, 0.0, below)
        + jnp.where(place == depth - 1, 0.0, above)
    )


def start_all(copies):
    for copy in copies:
        copy.start()


def wait_all(copies):
    for copy in copies:
        copy.wait()


def weight_copies(source, target, sems, first):
    channels = target.shape[1] // 3
    copies = []
    for tap in range(27):
        ab, c = tap // 3, tap % 3
        copies.append(
            pltpu.make_async_copy(
                source.at[tap],
                target.at[pl.ds(ab * channels, channels), pl.ds(c * channels, channels)],
                sems.at[first + tap],
            )
        )
    return copies


def coarse_kernel(sources, xor, *refs):
    coords = refs[:sources] if xor else refs[:1]
    refs = refs[sources:] if xor else refs[1:]
    (inp, x_first, x_second, y_first, y_second, weight) = refs[:6]
    outs = refs[6 : 6 + sources] if xor else refs[6:7]
    stats = refs[6 + len(outs)]
    padded, conv, wide, sems = refs[7 + len(outs) :]
    dx, dy, dz, channels = inp.shape
    slab = lax.axis_index("slab")
    sub = lax.axis_index("sub")
    rows = pl.ds(1, dy)
    x_even = lax.rem(slab, 2) == 0
    y_even = lax.rem(sub, 2) == 0
    xa = jnp.where(x_even, dx + 1, 0)
    xb = dx + 1 - xa
    ya = jnp.where(y_even, dy + 1, 0)
    yb = dy + 1 - ya
    moves = [
        (inp, padded.at[pl.ds(1, dx), rows]),
        (x_first, padded.at[xa, rows]),
        (x_second, padded.at[xb, rows]),
    ]
    for got, place in ((y_first, ya), (y_second, yb)):
        moves += [
            (got.at[0], padded.at[xa, place]),
            (got.at[pl.ds(1, dx)], padded.at[pl.ds(1, dx), place]),
            (got.at[dx + 1], padded.at[xb, place]),
        ]
    copies = [pltpu.make_async_copy(a, b, sems.at[i]) for i, (a, b) in enumerate(moves)]
    loads = weight_copies(weight, wide, sems, len(moves))
    start_all(loads)
    start_all(copies)
    wait_all(copies)
    wait_all(loads)
    total = jnp.zeros((8, channels), F32)
    for x in range(dx):
        taken = [
            padded[x + a, pl.ds(b, dy)].reshape(dy * dz, channels)
            for a in range(3)
            for b in range(3)
        ]
        value = shifted_sum(tap_sums(taken, wide[...]), dz, channels)
        conv[x] = value.reshape(dy, dz, channels)
        total = total + jnp.sum(value.reshape(-1, 8, channels), axis=0)
    mean = jnp.sum(total, axis=0, keepdims=True) / (dx * dy * dz)
    square = jnp.zeros((8, channels), F32)
    for x in range(dx):
        off = conv[x].reshape(-1, 8, channels) - mean[None]
        square = square + jnp.sum(off * off, axis=0)
    stats[0:1, :] = mean
    stats[1:2, :] = jnp.sum(square, axis=0, keepdims=True)
    edge = FB // 2
    for s in range(sources):
        wanted = coords[s] if xor else coords[0].at[s]
        seen = jnp.int32(0)
        where_y = [jnp.int32(0)] * MOST
        where_z = [jnp.int32(0)] * MOST
        for n in range(wanted.shape[0]):
            hit = wanted[n, 0] == slab
            y = wanted[n, 1] - sub * (dy // edge)
            for slot in range(MOST):
                here = jnp.logical_and(hit, seen == slot)
                where_y[slot] = jnp.where(here, y, where_y[slot])
                where_z[slot] = jnp.where(here, wanted[n, 2], where_z[slot])
            seen = seen + hit.astype(jnp.int32)
        out = outs[s] if xor else outs[0].at[s]
        for slot in range(MOST):
            for x in range(edge):
                for y in range(edge):
                    piece = conv[x, edge * where_y[slot] + y, pl.ds(edge * where_z[slot], edge), :]
                    out[slot, pl.ds((x * edge + y) * edge, edge), :] = piece


def group_sum(value, size):
    lanes = value.shape[-1]
    place = lax.broadcasted_iota(jnp.int32, value.shape, 1) % size
    total = value
    for step in range(1, size):
        total = total + jnp.where(place >= step, pltpu.roll(value, step, 1), 0.0)
        total = total + jnp.where(place + step < size, pltpu.roll(value, lanes - step, 1), 0.0)
    return total


def merge(means, squares, count):
    mean = sum(means) / len(means)
    square = sum(squares)
    for part in means:
        square = square + count * (part - mean) * (part - mean)
    return mean, square


def fine_kernel(cube_lists, stat_lists, cells, xor, *refs):
    coords, links = refs[:2]
    cubes = refs[2 : 2 + cube_lists]
    stats = refs[2 + cube_lists : 2 + cube_lists + stat_lists]
    gain, bias, lift, fine, weight, out = refs[2 + cube_lists + stat_lists : 8 + cube_lists + stat_lists]
    held, block, even, odd, wide, sems = refs[8 + cube_lists + stat_lists :]
    total, _, channels = fine.shape
    slab = lax.axis_index("slab")
    edge = FB // 2
    loads = weight_copies(weight, wide, sems, cube_lists)
    start_all(loads)
    moves = []
    for i, cube in enumerate(cubes):
        target = held.at[pl.ds(MOST * i, MOST)] if xor else held
        moves.append(pltpu.make_async_copy(cube, target, sems.at[i]))
    start_all(moves)
    size = channels // G
    mean, square = merge(
        [s[0:1, :] for s in stats], [s[1:2, :] for s in stats], float(cells)
    )
    cells = cells * stat_lists
    group_mean = group_sum(mean, size) / size
    off = mean - group_mean
    group_var = group_sum(square + cells * off * off, size) / (cells * size)
    scale = lax.rsqrt(group_var + EPS)
    duplicate = (
        lax.broadcasted_iota(jnp.int32, (2 * edge**3, edge**3), 1)
        == lax.broadcasted_iota(jnp.int32, (2 * edge**3, edge**3), 0) // FB * edge
        + lax.broadcasted_iota(jnp.int32, (2 * edge**3, edge**3), 0) % FB // 2
    ).astype(BF16)
    wait_all(moves)
    for n in range(total):
        holder = coords[n, 0]
        rank = jnp.int32(0)
        for m in range(n):
            rank = rank + (coords[m, 0] == holder).astype(jnp.int32)
        source = jnp.bitwise_xor(holder, slab) if xor else holder
        value = held[source * MOST + rank]
        normed = (value - group_mean) * scale * gain[...] + bias[...]
        acted = (normed / (1.0 + jnp.exp(-normed))).astype(BF16)
        lifted = jnp.dot(acted, lift[...], preferred_element_type=F32).astype(BF16)
        wider = jnp.dot(duplicate, lifted, preferred_element_type=F32)
        wider = wider.reshape(edge, edge, FB, channels)
        own = fine[n].astype(F32).reshape(FB, FB, FB, channels)
        for i in range(FB):
            for j in range(FB):
                summed = (own[i, j] + wider[i // 2, j // 2]).astype(BF16).astype(F32)
                block[n, i, j] = summed
    zero = jnp.zeros((FB, channels), F32)
    wait_all(loads)
    for n in range(total):
        picked = []
        for direction in range(4):
            target = links[n, direction]
            valid = (target >= 0).astype(F32)
            picked.append((lax.rem(jnp.maximum(target, 0), total), valid))
        for i in range(FB + 2):
            if 0 < i < FB + 1:
                line = [block[n, i - 1, j] for j in range(FB)]
                (low, low_on), (high, high_on) = picked[2], picked[3]
                line = [block[low, i - 1, FB - 1] * low_on] + line + [block[high, i - 1, 0] * high_on]
            else:
                (other, on) = picked[0] if i == 0 else picked[1]
                plane = FB - 1 if i == 0 else 0
                line = [zero] + [block[other, plane, j] * on for j in range(FB)] + [zero]
            for j in range(0, FB, 2):
                even[i, j // 2] = jnp.concatenate(line[j + 1 : j + 3], axis=0).astype(BF16)
            for j in range(0, FB + 2, 2):
                odd[i, j // 2] = jnp.concatenate(line[j : j + 2], axis=0).astype(BF16)
        taken = []
        for a in range(3):
            for b in range(3):
                if b == 1:
                    part = even[pl.ds(a, FB)]
                else:
                    part = odd[pl.ds(a, FB), pl.ds(b // 2, FB // 2)]
                taken.append(part.reshape(FB**3, channels))
        value = shifted_sum(tap_sums(taken, wide[...]), FB, channels)
        value = value + block[n].reshape(FB**3, channels)
        out[n] = value.astype(BF16)


def body(
    coarse_in,
    coarse_weight,
    norm_gain,
    norm_bias,
    lift_weight,
    fine_input,
    block_coords,
    neighbours,
    fine_weight,
):
    dx, dy, dz, channels = coarse_in.shape
    slabs, subs = lax.axis_size("slab"), lax.axis_size("sub")
    slab, sub = lax.axis_index("slab"), lax.axis_index("sub")
    total = block_coords.shape[0]
    xor = slabs == 4
    edge = FB // 2
    if xor:
        near = lax.ppermute(block_coords, "slab", xor_links(slabs, 1))
        both = jnp.stack([block_coords, near])
        far = lax.ppermute(both, "slab", xor_links(slabs, 2))
        asked = [block_coords, near, far[0], far[1]]
    else:
        asked = [lax.all_gather(block_coords, "slab", axis=0)]
    x_even, y_even = slab % 2 == 0, sub % 2 == 0
    last, first = coarse_in[dx - 1], coarse_in[0]
    x_first = lax.ppermute(jnp.where(x_even, last, first), "slab", pairs(slabs, 0))
    x_second = lax.ppermute(jnp.where(x_even, first, last), "slab", pairs(slabs, 1))
    low = jnp.concatenate([x_first[None, 0], coarse_in[:, 0], x_second[None, 0]])
    high = jnp.concatenate([x_first[None, dy - 1], coarse_in[:, dy - 1], x_second[None, dy - 1]])
    y_first = lax.ppermute(jnp.where(y_even, high, low), "sub", pairs(subs, 0))
    y_second = lax.ppermute(jnp.where(y_even, low, high), "sub", pairs(subs, 1))

    smem = pl.BlockSpec(memory_space=pltpu.SMEM)
    vmem = pl.BlockSpec(memory_space=pltpu.VMEM)
    hbm = pl.BlockSpec(memory_space=pl.ANY)
    piece = (MOST, edge**3, channels)
    if xor:
        shapes = [jax.ShapeDtypeStruct(piece, F32)] * slabs
    else:
        shapes = [jax.ShapeDtypeStruct((slabs,) + piece, F32)]
    results = pl.pallas_call(
        functools.partial(coarse_kernel, slabs, xor),
        out_shape=shapes + [jax.ShapeDtypeStruct((8, channels), F32)],
        in_specs=[smem] * len(asked) + [hbm] * 6,
        out_specs=[vmem] * (len(shapes) + 1),
        scratch_shapes=[
            pltpu.VMEM((dx + 2, dy + 2, dz, channels), BF16),
            pltpu.VMEM((dx, dy, dz, channels), F32),
            pltpu.VMEM((9 * channels, 3 * channels), BF16),
            pltpu.SemaphoreType.DMA((9 + 27,)),
        ],
        name="coarse",
    )(*asked, coarse_in, x_first, x_second, y_first, y_second, coarse_weight)
    sent, stats = results[:-1], results[-1]
    cells = dx * dy * dz
    if xor:
        replies = [sent[0]]
        parts = [stats]
        for distance in range(1, slabs):
            parts.append(lax.ppermute(stats, "slab", xor_links(slabs, distance)))
            replies.append(lax.ppermute(sent[distance], "slab", xor_links(slabs, distance)))
    else:
        replies = [
            lax.all_to_all(sent[0], "slab", split_axis=0, concat_axis=0, tiled=True).reshape(
                slabs * MOST, edge**3, channels
            )
        ]
        parts = list(lax.all_gather(stats, "slab", axis=0))
    mean, square = merge([p[0:1] for p in parts], [p[1:2] for p in parts], float(cells))
    cells = cells * slabs
    merged = jnp.concatenate([mean, square])
    if subs == 4:
        lines = [merged] + [
            lax.ppermute(merged, "sub", xor_links(subs, distance)) for distance in range(1, subs)
        ]
    else:
        lines = list(lax.all_gather(merged, "sub", axis=0))

    return pl.pallas_call(
        functools.partial(fine_kernel, len(replies), len(lines), cells, xor),
        out_shape=jax.ShapeDtypeStruct(fine_input.shape, BF16),
        in_specs=[smem] * 2 + [hbm] * len(replies) + [vmem] * (len(lines) + 4) + [hbm],
        out_specs=vmem,
        scratch_shapes=[
            pltpu.VMEM((slabs * MOST, edge**3, channels), F32),
            pltpu.VMEM((total, FB, FB, FB, channels), F32),
            pltpu.VMEM((FB + 2, FB // 2, 2 * FB, channels), BF16),
            pltpu.VMEM((FB + 2, FB // 2 + 1, 2 * FB, channels), BF16),
            pltpu.VMEM((9 * channels, 3 * channels), BF16),
            pltpu.SemaphoreType.DMA((len(replies) + 27,)),
        ],
        name="fine",
    )(
        block_coords,
        neighbours,
        *replies,
        *lines,
        norm_gain.reshape(1, channels),
        norm_bias.reshape(1, channels),
        lift_weight,
        fine_input,
        fine_weight,
    )


def solution(mesh):
    in_specs = (
        P(("scene", "slab"), "sub", None, None),
        P(),
        P(),
        P(),
        P(),
        P(("scene", "slab", "sub"), None, None),
        P(("scene", "slab", "sub"), None),
        P(("scene", "slab", "sub"), None),
        P(),
    )
    out_specs = P(("scene", "slab", "sub"), None, None)
    return jax.shard_map(body, mesh=mesh, in_specs=in_specs, out_specs=out_specs, check_vma=False)
```

```python
import functools

import jax
import jax.numpy as jnp
from jax import lax
from jax.experimental import pallas as pl
from jax.experimental.pallas import tpu as pltpu
from jax.sharding import PartitionSpec as P

G = 32
FB = 8
EDGE = FB // 2
MOST = 2
EPS = 1e-05
F32 = jnp.float32
BF16 = jnp.bfloat16


def pairs(count, odd):
    links = []
    for i in range(odd, count - 1, 2):
        links += [(i, i + 1), (i + 1, i)]
    return links


def xor_links(count, distance):
    return [(i, i ^ distance) for i in range(count)]


def wide_weight(weight):
    return jnp.concatenate(
        [
            jnp.concatenate([weight[3 * ab + c] for c in range(3)], axis=1)
            for ab in range(9)
        ],
        axis=0,
    )


def shifted_sum(sums, depth, channels):
    rows = sums.shape[0]
    place = lax.broadcasted_iota(jnp.int32, (rows, channels), 0) % depth
    below = pltpu.roll(sums[:, :channels], 1, 0)
    above = pltpu.roll(sums[:, 2 * channels :], rows - 1, 0)
    return (
        sums[:, channels : 2 * channels]
        + jnp.where(place == 0, 0.0, below)
        + jnp.where(place == depth - 1, 0.0, above)
    )


def neighbour(links, n, direction, total):
    target = links[n, direction]
    return lax.rem(jnp.maximum(target, 0), total), target >= 0


def fold_weights(weight, out):
    channels = weight.shape[1]
    taps = (((0,), (1, 2)), ((0, 1), (2,)))
    for p in range(2):
        for q in range(2):
            for a in range(2):
                for b in range(2):
                    sums = []
                    for c in range(3):
                        parts = [
                            weight[9 * i + 3 * j + c].astype(F32)
                            for i in taps[p][a]
                            for j in taps[q][b]
                        ]
                        sums.append(functools.reduce(jnp.add, parts))
                    kinds = [sums[1] + sums[2], sums[0], sums[0] + sums[1], sums[2]]
                    rows = pl.ds((2 * a + b) * channels, channels)
                    for k, kind in enumerate(kinds):
                        out[2 * p + q, rows, pl.ds(k * channels, channels)] = kind.astype(BF16)


def parity(name, length):
    return jnp.where(lax.rem(lax.axis_index(name), 2) == 0, length - 1, 0)


def send_kernel(inp, coords, links, send_a, send_b, row_a, row_b, coords_out, links_out, note, sems):
    dx, dy = inp.shape[:2]
    xa, ya = parity("slab", dx), parity("sub", dy)
    moves = [
        (coords, coords_out),
        (inp.at[xa], send_a.at[pl.ds(0, dy)]),
        (inp.at[dx - 1 - xa], send_b),
        (inp.at[:, ya], row_a),
        (inp.at[:, dy - 1 - ya], row_b),
        (links, links_out),
    ]
    copies = [pltpu.make_async_copy(a, b, sems.at[i]) for i, (a, b) in enumerate(moves)]
    for copy in copies:
        copy.start()
    note[...] = jnp.zeros_like(note)
    copies[0].wait()
    note[pl.ds(0, coords.shape[0]), pl.ds(0, coords.shape[1])] = coords_out[...]
    send_a[dy] = note[...].astype(F32).astype(BF16)
    for copy in copies[1:]:
        copy.wait()


def line_kernel(x_first, x_second, row_a, row_b, line_a, line_b):
    dx, dy = row_a.shape[0], x_second.shape[0]
    ya = parity("sub", dy)
    for place, row, line in ((ya, row_a, line_a), (dy - 1 - ya, row_b, line_b)):
        line[0] = x_first[place]
        line[pl.ds(1, dx)] = row[...]
        line[dx + 1] = x_second[place]


def fine_kernel(first, count, role, *refs):
    loads = []
    if role == "load":
        links, fine_from, weight_from, inp = refs[:4]
        out, fine, weight, padded, even, odd, sems = refs[4:]
        dx, dy = inp.shape[:2]
        moves = [
            (fine_from, fine),
            (weight_from, weight),
            (inp, padded.at[pl.ds(1, dx), pl.ds(1, dy)]),
        ]
        loads = [pltpu.make_async_copy(a, b, sems.at[i]) for i, (a, b) in enumerate(moves)]
        for load in loads:
            load.start()
        loads[0].wait()
    elif role == "fold":
        links, fine, weight, _, out, folded, even, odd = refs
        fold_weights(weight, folded)
    else:
        links, fine, weight, _, out, even, odd = refs
    total, _, channels = fine.shape
    tile = 2 * FB
    lines = FB // 2

    def plane(n, i):
        return fine[n, pl.ds(i * FB * FB, FB * FB), :].reshape(lines, tile, channels)

    zero = jnp.zeros((FB, channels), F32)
    for slot in range(count):
        n = first + slot
        sides = [neighbour(links, n, direction, total) for direction in range(4)]
        for i in range(-1, FB + 1):
            if 0 <= i < FB:
                here = plane(n, i)
                (low, low_on), (high, high_on) = sides[2], sides[3]
                before = fine[low, pl.ds(i * FB * FB + FB * FB - tile, tile), :].astype(F32)
                after = fine[high, pl.ds(i * FB * FB, tile), :].astype(F32)
                before = jnp.where(low_on, before[FB:], 0.0)
                after = jnp.where(high_on, after[:FB], 0.0)
            else:
                other, on = sides[0] if i < 0 else sides[1]
                here = plane(other, FB - 1 if i < 0 else 0)
                here = jnp.where(on, here, jnp.zeros_like(here))
                before = after = zero
            even[slot, i + 1] = here
            wide = here.astype(F32)
            halves = [before]
            for line in range(lines):
                halves += [wide[line, :FB], wide[line, FB:]]
            halves.append(after)
            for line in range(lines + 1):
                odd[slot, i + 1, line] = jnp.concatenate(
                    halves[2 * line : 2 * line + 2], axis=0
                ).astype(BF16)
        if role == "load" and slot == 0:
            loads[1].wait()
        taken = []
        for a in range(3):
            for b in range(3):
                if b == 1:
                    part = even[slot, pl.ds(a, FB)]
                else:
                    part = odd[slot, pl.ds(a, FB), pl.ds(b // 2, lines)]
                taken.append(part.reshape(FB**3, channels))
        sums = jnp.dot(
            jnp.concatenate(taken, axis=1), wide_weight(weight), preferred_element_type=F32
        )
        out[slot] = shifted_sum(sums, FB, channels)
    for load in loads[2:]:
        load.wait()


def coarse_kernel(sources, xor, cells_shape, total_blocks, *refs):
    own, far = refs[:2]
    _, x_first, x_second, y_first, y_second, weight = refs[2:8]
    outs = refs[8:-5]
    padded, conv, notes, wanted, sems = refs[-5:]
    dx, dy, dz = cells_shape
    asked = [own[dy], x_first[dy], far[0], far[1]] if xor else [far[s] for s in range(sources)]
    for s, note in enumerate(asked):
        notes[s] = note.astype(F32).astype(jnp.int32)
    noted = pltpu.make_async_copy(notes, wanted, sems.at[2])
    noted.start()
    channels = padded.shape[-1]
    slab = lax.axis_index("slab")
    sub = lax.axis_index("sub")
    rows = pl.ds(1, dy)
    xa = jnp.where(lax.rem(slab, 2) == 0, dx + 1, 0)
    xb = dx + 1 - xa
    ya = jnp.where(lax.rem(sub, 2) == 0, dy + 1, 0)
    yb = dy + 1 - ya
    moves = [(x_first.at[pl.ds(0, dy)], padded.at[xa, rows]), (x_second, padded.at[xb, rows])]
    copies = [pltpu.make_async_copy(a, b, sems.at[i]) for i, (a, b) in enumerate(moves)]
    for copy in copies:
        copy.start()
    for got, place in ((y_first, ya), (y_second, yb)):
        padded[xa, place] = got[0]
        for x in range(dx):
            padded[1 + x, place] = got[1 + x]
        padded[xb, place] = got[dx + 1]
    for copy in copies:
        copy.wait()
    total = jnp.zeros((8, channels), F32)
    for x in range(dx):
        taken = [
            padded[x + a, pl.ds(b, dy)].reshape(dy * dz, channels)
            for a in range(3)
            for b in range(3)
        ]
        sums = jnp.dot(
            jnp.concatenate(taken, axis=1), wide_weight(weight), preferred_element_type=F32
        )
        value = shifted_sum(sums, dz, channels)
        conv[x] = value.reshape(dy, dz, channels)
        total = total + jnp.sum(value.reshape(-1, 8, channels), axis=0)
    mean = jnp.sum(total, axis=0, keepdims=True) / (dx * dy * dz)
    square = jnp.zeros((8, channels), F32)
    for x in range(dx):
        off = conv[x].reshape(-1, 8, channels) - mean[None]
        square = square + jnp.sum(off * off, axis=0)
    square = jnp.sum(square, axis=0, keepdims=True)
    noted.wait()
    for s in range(sources):
        seen = jnp.int32(0)
        where_y = [jnp.int32(0)] * MOST
        where_z = [jnp.int32(0)] * MOST
        for n in range(total_blocks):
            hit = wanted[s, 0, n] == slab
            y = wanted[s, 1, n] - sub * (dy // EDGE)
            for slot in range(MOST):
                here = jnp.logical_and(hit, seen == slot)
                where_y[slot] = jnp.where(here, y, where_y[slot])
                where_z[slot] = jnp.where(here, wanted[s, 2, n], where_z[slot])
            seen = seen + hit.astype(jnp.int32)
        out = outs[s] if xor else outs[0].at[s]
        for slot in range(MOST):
            for x in range(EDGE):
                for y in range(EDGE):
                    piece = conv[x, EDGE * where_y[slot] + y, pl.ds(EDGE * where_z[slot], EDGE), :]
                    out[pl.ds(slot * EDGE**3 + (x * EDGE + y) * EDGE, EDGE), :] = piece
        out[pl.ds(MOST * EDGE**3, 1), :] = mean
        out[pl.ds(MOST * EDGE**3 + 1, 1), :] = square


def group_sum(value, size):
    lanes = value.shape[-1]
    place = lax.broadcasted_iota(jnp.int32, value.shape, 1) % size
    total = value
    for step in range(1, size):
        total = total + jnp.where(place >= step, pltpu.roll(value, step, 1), 0.0)
        total = total + jnp.where(place + step < size, pltpu.roll(value, lanes - step, 1), 0.0)
    return total


def merge(means, squares, count):
    mean = sum(means) / len(means)
    square = sum(squares)
    for part in means:
        square = square + count * (part - mean) * (part - mean)
    return mean, square


def final_kernel(cube_lists, stat_lists, cells, xor, *refs):
    coords, links = refs[:2]
    cubes = refs[2 : 2 + cube_lists]
    stats = refs[2 + cube_lists : 2 + cube_lists + stat_lists]
    rest = refs[2 + cube_lists + stat_lists :]
    gain, bias, lift, fine, folded = rest[:5]
    pieces, out_to = rest[5:-9], rest[-9]
    held, acted, lifted, twice, frame, spread, out, sems = rest[-8:]
    total, _, channels = fine.shape
    slab = lax.axis_index("slab")
    volume = EDGE**3
    for i, cube in enumerate(cubes):
        for slot in range(MOST):
            if xor:
                held[MOST * i + slot] = cube[pl.ds(slot * volume, volume), :]
            else:
                for s in range(cube.shape[0]):
                    held[MOST * s + slot] = cube[s, pl.ds(slot * volume, volume), :]
    size = channels // G
    mean, square = merge(
        [s[0:1, :] for s in stats], [s[1:2, :] for s in stats], float(cells)
    )
    cells = cells * stat_lists
    group_mean = group_sum(mean, size) / size
    off = mean - group_mean
    group_var = group_sum(square + cells * off * off, size) / (cells * size)
    scale = lax.rsqrt(group_var + EPS)
    for n in range(total):
        holder = coords[0, n]
        rank = jnp.int32(0)
        for m in range(n):
            rank = rank + (coords[0, m] == holder).astype(jnp.int32)
        source = jnp.bitwise_xor(holder, slab) if xor else holder
        value = held[source * MOST + rank]
        normed = (value - group_mean) * scale * gain[...] + bias[...]
        acted[pl.ds(n * volume, volume), :] = (normed / (1.0 + jnp.exp(-normed))).astype(BF16)
    rounded = jnp.dot(acted[...], lift[...], preferred_element_type=F32).astype(BF16).astype(F32)
    rows = total * volume
    twice[pl.ds(0, rows, stride=2), :] = rounded
    twice[pl.ds(1, rows, stride=2), :] = rounded
    flat = EDGE * EDGE
    lifted[...] = rounded.reshape(total, EDGE, flat, channels)
    place = lax.broadcasted_iota(jnp.int32, (flat, channels), 0)
    for n in range(total):
        sides = [neighbour(links, n, direction, total) for direction in range(4)]
        for i in range(-1, EDGE + 1):
            if 0 <= i < EDGE:
                here = lifted[n, i]
                (low, low_on), (high, high_on) = sides[2], sides[3]
                before = jnp.where(low_on, lifted[low, i], 0.0)
                after = jnp.where(high_on, lifted[high, i], 0.0)
                before = pltpu.roll(before, EDGE, 0)
                after = pltpu.roll(after, flat - EDGE, 0)
            else:
                other, on = sides[0] if i < 0 else sides[1]
                here = jnp.where(on, lifted[other, EDGE - 1 if i < 0 else 0], 0.0)
                before = after = jnp.zeros_like(here)
            frame[0, n, i + 1] = jnp.where(
                place < EDGE, before, pltpu.roll(here, EDGE, 0)
            ).astype(BF16)
            frame[1, n, i + 1] = here.astype(BF16)
            frame[2, n, i + 1] = jnp.where(
                place >= flat - EDGE, after, pltpu.roll(here, flat - EDGE, 0)
            ).astype(BF16)
    level = lax.broadcasted_iota(jnp.int32, (rows, channels), 0) % EDGE
    for p in range(2):
        for q in range(2):
            taken = [
                frame[q + b, :, pl.ds(p + a, EDGE)].reshape(rows, channels)
                for a in range(2)
                for b in range(2)
            ]
            sums = jnp.dot(
                jnp.concatenate(taken, axis=1), folded[2 * p + q], preferred_element_type=F32
            )
            below = pltpu.roll(sums[:, channels : 2 * channels], 1, 0)
            above = pltpu.roll(sums[:, 3 * channels :], rows - 1, 0)
            even = sums[:, :channels] + jnp.where(level == 0, 0.0, below)
            odd = sums[:, 2 * channels : 3 * channels] + jnp.where(level == EDGE - 1, 0.0, above)
            spread[2 * p + q, pl.ds(0, rows, stride=2), :] = even
            spread[2 * p + q, pl.ds(1, rows, stride=2), :] = odd
    copies = []
    whole = [piece.at[n] for piece in pieces for n in range(piece.shape[0])]
    for n, part in enumerate(whole):
        for i in range(FB):
            for j in range(0, FB, 2):
                cell = pl.ds(((n * EDGE + i // 2) * EDGE + j // 2) * FB, FB)
                pair = pl.ds((i * FB + j) * FB, 2 * FB)
                up = twice[cell, :]
                raised = jnp.concatenate([up, up], axis=0)
                own = (fine[n, pair, :].astype(F32) + raised).astype(BF16).astype(F32)
                conv = jnp.concatenate(
                    [spread[2 * (i % 2), cell, :], spread[2 * (i % 2) + 1, cell, :]], axis=0
                )
                out[n, pair, :] = (own + part[pair, :] + conv).astype(BF16)
        copies.append(pltpu.make_async_copy(out.at[n], out_to.at[n], sems.at[n]))
        copies[-1].start()
    for copy in copies:
        copy.wait()


SMEM = pl.BlockSpec(memory_space=pltpu.SMEM)
VMEM = pl.BlockSpec(memory_space=pltpu.VMEM)
HBM = pl.BlockSpec(memory_space=pl.ANY)


def limit(mib):
    return pltpu.CompilerParams(vmem_limit_bytes=mib * 2**20)


def fine_part(links, fine, weight, after, first, count, role):
    total, cells, channels = fine.shape
    shapes = [jax.ShapeDtypeStruct((count, cells, channels), F32)]
    specs, sems = [SMEM, VMEM, VMEM, HBM], []
    if role == "fold":
        shapes.append(jax.ShapeDtypeStruct((4, 4 * channels, 4 * channels), BF16))
    if role == "load":
        dx, dy, dz, _ = after.shape
        extra = [fine.shape, weight.shape, (dx + 2, dy + 2, dz, channels)]
        shapes += [jax.ShapeDtypeStruct(shape, BF16) for shape in extra]
        specs = [SMEM] + [pl.BlockSpec(memory_space=pltpu.HBM)] * 3
        sems = [pltpu.SemaphoreType.DMA((len(extra),))]
        fine, weight, after = (
            pltpu.with_memory_space_constraint(x, pltpu.HBM) for x in (fine, weight, after)
        )
    return pl.pallas_call(
        functools.partial(fine_kernel, first, count, role),
        out_shape=shapes,
        in_specs=specs,
        out_specs=[VMEM] * len(shapes),
        scratch_shapes=[
            pltpu.VMEM((count, FB + 2, FB // 2, 2 * FB, channels), BF16),
            pltpu.VMEM((count, FB + 2, FB // 2 + 1, 2 * FB, channels), BF16),
        ]
        + sems,
        compiler_params=limit(18),
        cost_estimate=pl.CostEstimate(
            flops=2 * 27 * count * cells * channels * channels,
            bytes_accessed=4 * count * cells * channels,
            transcendentals=0,
        ),
        name="fine_part",
    )(links, fine, weight, after)


def body(
    coarse_in,
    coarse_weight,
    norm_gain,
    norm_bias,
    lift_weight,
    fine_input,
    block_coords,
    neighbours,
    fine_weight,
):
    dx, dy, dz, channels = coarse_in.shape
    slabs, subs = lax.axis_size("slab"), lax.axis_size("sub")
    total = block_coords.shape[0]
    xor = slabs == 4
    coords = block_coords.T
    send_a, send_b, row_a, row_b, coords, links = pl.pallas_call(
        send_kernel,
        out_shape=[
            jax.ShapeDtypeStruct((dy + 1, dz, channels), BF16),
            jax.ShapeDtypeStruct((dy, dz, channels), BF16),
            jax.ShapeDtypeStruct((dx, dz, channels), BF16),
            jax.ShapeDtypeStruct((dx, dz, channels), BF16),
            jax.ShapeDtypeStruct(coords.shape, jnp.int32),
            jax.ShapeDtypeStruct(neighbours.shape, jnp.int32),
        ],
        in_specs=[pl.BlockSpec(memory_space=pltpu.HBM)] * 3,
        out_specs=[VMEM] * 6,
        scratch_shapes=[pltpu.VMEM((dz, channels), jnp.int32), pltpu.SemaphoreType.DMA((6,))],
        compiler_params=limit(4),
        name="send",
    )(*(pltpu.with_memory_space_constraint(x, pltpu.HBM) for x in (coarse_in, coords, neighbours)))
    x_first = lax.ppermute(send_a, "slab", pairs(slabs, 0))
    x_second = lax.ppermute(send_b, "slab", pairs(slabs, 1))
    if xor:
        both = jnp.stack([send_a[dy], x_first[dy]])
        far = lax.ppermute(both, "slab", xor_links(slabs, 2))
    else:
        far = lax.all_gather(send_a[dy], "slab", axis=0)
    shares = [0, total // 4, total * 3 // 4, total]
    pieces = []

    def fill(index, after, waiting, role="plain"):
        begin = shares[index]
        made = fine_part(links, fine, weight, after, begin, shares[index + 1] - begin, role)
        made, waiting = lax.optimization_barrier((made, waiting))
        pieces.append(made[0])
        return made[1:], waiting

    fine, weight = fine_input, fine_weight
    made, (x_first, x_second, far) = fill(0, coarse_in, (x_first, x_second, far), "load")
    fine, weight, padded = made
    line_a, line_b = pl.pallas_call(
        line_kernel,
        out_shape=[jax.ShapeDtypeStruct((dx + 2, dz, channels), BF16)] * 2,
        in_specs=[VMEM] * 4,
        out_specs=[VMEM] * 2,
        compiler_params=limit(4),
        name="line",
    )(x_first, x_second, row_a, row_b)
    y_first = lax.ppermute(line_a, "sub", pairs(subs, 0))
    y_second = lax.ppermute(line_b, "sub", pairs(subs, 1))

    piece = (MOST * EDGE**3 + 8, channels)
    if xor:
        shapes = [jax.ShapeDtypeStruct(piece, F32)] * slabs
    else:
        shapes = [jax.ShapeDtypeStruct((slabs,) + piece, F32)]
    results = pl.pallas_call(
        functools.partial(coarse_kernel, slabs, xor, (dx, dy, dz), total),
        out_shape=shapes + [jax.ShapeDtypeStruct(padded.shape, BF16)],
        in_specs=[VMEM] * 8,
        out_specs=[VMEM] * (len(shapes) + 1),
        scratch_shapes=[
            pltpu.VMEM((dx, dy, dz, channels), F32),
            pltpu.VMEM((slabs, dz, channels), jnp.int32),
            pltpu.SMEM((slabs, dz, channels), jnp.int32),
            pltpu.SemaphoreType.DMA((3,)),
        ],
        input_output_aliases={2: len(shapes)},
        compiler_params=limit(12),
        name="coarse",
    )(send_a, far, padded, x_first, x_second, y_first, y_second, coarse_weight)
    sent = results[:-1]
    cells = dx * dy * dz
    row = MOST * EDGE**3
    if xor:
        replies = [sent[0]] + [
            lax.ppermute(sent[distance], "slab", xor_links(slabs, distance))
            for distance in range(1, slabs)
        ]
        parts = [r[row : row + 2] for r in replies]
    else:
        replies = [lax.all_to_all(sent[0], "slab", split_axis=0, concat_axis=0, tiled=True)]
        parts = [replies[0][s, row : row + 2] for s in range(slabs)]
    _, parts = fill(1, sent[0], parts)
    mean, square = merge([p[0:1] for p in parts], [p[1:2] for p in parts], float(cells))
    cells = cells * slabs
    merged = jnp.concatenate([mean, square])
    if subs == 4:
        lines = [merged] + [
            lax.ppermute(merged, "sub", xor_links(subs, distance)) for distance in range(1, subs)
        ]
    else:
        lines = list(lax.all_gather(merged, "sub", axis=0))
    (folded,), lines = fill(2, merged, lines, "fold")

    volume = EDGE**3
    return pl.pallas_call(
        functools.partial(final_kernel, len(replies), len(lines), cells, xor),
        out_shape=jax.ShapeDtypeStruct(fine_input.shape, BF16),
        in_specs=[SMEM] * 2 + [VMEM] * (len(replies) + len(lines) + 5 + len(pieces)),
        out_specs=HBM,
        scratch_shapes=[
            pltpu.VMEM((slabs * MOST, volume, channels), F32),
            pltpu.VMEM((total * volume, channels), BF16),
            pltpu.VMEM((total, EDGE, EDGE * EDGE, channels), F32),
            pltpu.VMEM((2 * total * volume, channels), F32),
            pltpu.VMEM((3, total, EDGE + 2, EDGE * EDGE, channels), BF16),
            pltpu.VMEM((4, 2 * total * volume, channels), F32),
            pltpu.VMEM(fine_input.shape, BF16),
            pltpu.SemaphoreType.DMA((total,)),
        ],
        compiler_params=limit(18),
        name="final",
    )(
        coords,
        links,
        *replies,
        *lines,
        norm_gain.reshape(1, channels),
        norm_bias.reshape(1, channels),
        lift_weight,
        fine,
        folded,
        *pieces,
    )


def solution(mesh):
    in_specs = (
        P(("scene", "slab"), "sub", None, None),
        P(),
        P(),
        P(),
        P(),
        P(("scene", "slab", "sub"), None, None),
        P(("scene", "slab", "sub"), None),
        P(("scene", "slab", "sub"), None),
        P(),
    )
    out_specs = P(("scene", "slab", "sub"), None, None)
    return jax.shard_map(body, mesh=mesh, in_specs=in_specs, out_specs=out_specs, check_vma=False)
```

```python
import functools

import jax
import jax.numpy as jnp
from jax import lax
from jax.experimental import pallas as pl
from jax.experimental.pallas import tpu as pltpu
from jax.sharding import PartitionSpec as P


G = 32
FB = 8
EDGE = FB // 2
MOST = 2
TAIL = 16
SENT = jnp.bfloat16
EPS = 1e-05
F32 = jnp.float32
BF16 = jnp.bfloat16


def pairs(count, odd):
    links = []
    for i in range(odd, count - 1, 2):
        links += [(i, i + 1), (i + 1, i)]
    return links


def xor_links(count, distance):
    return [(i, i ^ distance) for i in range(count)]


def wide_weight(weight):
    return jnp.concatenate(
        [
            jnp.concatenate([weight[3 * ab + c] for c in range(3)], axis=1)
            for ab in range(9)
        ],
        axis=0,
    )


def shifted_sum(sums, depth, channels):
    rows = sums.shape[0]
    place = lax.broadcasted_iota(jnp.int32, (rows, channels), 0) % depth
    below = pltpu.roll(sums[:, :channels], 1, 0)
    above = pltpu.roll(sums[:, 2 * channels :], rows - 1, 0)
    return (
        sums[:, channels : 2 * channels]
        + jnp.where(place == 0, 0.0, below)
        + jnp.where(place == depth - 1, 0.0, above)
    )


def neighbour(links, n, direction, total):
    target = links[n, direction]
    return lax.rem(jnp.maximum(target, 0), total), target >= 0


def fold_weights(weight, out):
    channels = weight.shape[1]
    taps = (((0,), (1, 2)), ((0, 1), (2,)))
    for p in range(2):
        for q in range(2):
            for a in range(2):
                for b in range(2):
                    sums = []
                    for c in range(3):
                        parts = [
                            weight[9 * i + 3 * j + c].astype(F32)
                            for i in taps[p][a]
                            for j in taps[q][b]
                        ]
                        sums.append(functools.reduce(jnp.add, parts))
                    kinds = [sums[1] + sums[2], sums[0], sums[0] + sums[1], sums[2]]
                    rows = pl.ds((2 * a + b) * channels, channels)
                    for k, kind in enumerate(kinds):
                        out[2 * p + q, rows, pl.ds(k * channels, channels)] = kind.astype(BF16)


def parity(name, length):
    return jnp.where(lax.rem(lax.axis_index(name), 2) == 0, length - 1, 0)


def send_kernel(inp, coords, links, send_a, send_b, row_a, row_b, coords_out, links_out, note, sems):
    dx, dy = inp.shape[:2]
    xa, ya = parity("slab", dx), parity("sub", dy)
    moves = [
        (coords, coords_out),
        (inp.at[xa], send_a.at[pl.ds(0, dy)]),
        (inp.at[dx - 1 - xa], send_b.at[pl.ds(0, dy)]),
        (inp.at[:, ya], row_a),
        (inp.at[:, dy - 1 - ya], row_b),
        (links, links_out),
    ]
    copies = [pltpu.make_async_copy(a, b, sems.at[i]) for i, (a, b) in enumerate(moves)]
    for copy in copies:
        copy.start()
    note[...] = jnp.zeros_like(note)
    copies[0].wait()
    note[pl.ds(0, coords.shape[0]), pl.ds(0, coords.shape[1])] = coords_out[...] + 1
    send_a[dy] = note[...].astype(F32).astype(BF16)
    send_b[dy] = send_a[dy]
    send_b[dy + 1] = jnp.zeros_like(send_a[dy])
    for copy in copies[1:]:
        copy.wait()


def relay_kernel(x_first, _, send_b):
    send_b[send_b.shape[0] - 1] = x_first[x_first.shape[0] - 1]


def inside(xor, slabs):
    slab = lax.axis_index("slab")
    return jnp.logical_or(not xor, jnp.logical_and(slab > 0, slab < slabs - 1))


def line_kernel(slabs, xor, x_first, x_second, row_a, row_b, line_a, line_b):
    dx, dy = row_a.shape[0], x_first.shape[0] - 1
    has = inside(xor, slabs)
    ya = parity("sub", dy)
    for place, row, line in ((ya, row_a, line_a), (dy - 1 - ya, row_b, line_b)):
        line[0] = x_first[place]
        line[pl.ds(1, dx)] = row[...]
        line[dx + 1] = jnp.where(has, x_second[place], jnp.zeros_like(x_second[place]))


def fine_kernel(first, count, role, *refs):
    loads = []
    if role == "load":
        links, fine_from, weight_from, _, inp = refs[:5]
        out, fine, weight, padded, folded, even, odd, sems = refs[5:]
        dx, dy = inp.shape[:2]
        moves = [
            (fine_from, fine),
            (weight_from, weight),
            (inp, padded.at[pl.ds(1, dx), pl.ds(1, dy)]),
        ]
        loads = [pltpu.make_async_copy(a, b, sems.at[i]) for i, (a, b) in enumerate(moves)]
        for load in loads:
            load.start()
        for y in (0, dy + 1):
            padded[:, y] = jnp.zeros((dx + 2,) + padded.shape[2:], BF16)
        loads[0].wait()
    else:
        links, fine, weight, _, out, even, odd = refs
    total, _, channels = fine.shape
    tile = 2 * FB
    lines = FB // 2

    def plane(n, i):
        return fine[n, pl.ds(i * FB * FB, FB * FB), :].reshape(lines, tile, channels)

    zero = jnp.zeros((FB, channels), F32)
    for slot in range(count):
        n = first + slot
        sides = [neighbour(links, n, direction, total) for direction in range(4)]
        for i in range(-1, FB + 1):
            if 0 <= i < FB:
                here = plane(n, i)
                (low, low_on), (high, high_on) = sides[2], sides[3]
                before = fine[low, pl.ds(i * FB * FB + FB * FB - tile, tile), :].astype(F32)
                after = fine[high, pl.ds(i * FB * FB, tile), :].astype(F32)
                before = jnp.where(low_on, before[FB:], 0.0)
                after = jnp.where(high_on, after[:FB], 0.0)
            else:
                other, on = sides[0] if i < 0 else sides[1]
                here = plane(other, FB - 1 if i < 0 else 0)
                here = jnp.where(on, here, jnp.zeros_like(here))
                before = after = zero
            even[slot, i + 1] = here
            wide = here.astype(F32)
            halves = [before]
            for line in range(lines):
                halves += [wide[line, :FB], wide[line, FB:]]
            halves.append(after)
            for line in range(lines + 1):
                odd[slot, i + 1, line] = jnp.concatenate(
                    halves[2 * line : 2 * line + 2], axis=0
                ).astype(BF16)
        if role == "load" and slot == 0:
            loads[1].wait()
        taken = []
        for a in range(3):
            for b in range(3):
                if b == 1:
                    part = even[slot, pl.ds(a, FB)]
                else:
                    part = odd[slot, pl.ds(a, FB), pl.ds(b // 2, lines)]
                taken.append(part.reshape(FB**3, channels))
        sums = jnp.dot(
            jnp.concatenate(taken, axis=1), wide_weight(weight), preferred_element_type=F32
        )
        out[slot] = shifted_sum(sums, FB, channels)
    if role == "load":
        fold_weights(weight, folded)
    for load in loads[2:]:
        load.wait()


def choose(notes, y_cubes):
    rows = [jnp.concatenate([note[k : k + 1] for note in notes], axis=0) for k in range(3)]
    lane = lax.broadcasted_iota(jnp.int32, rows[0].shape, 1)
    slab = lax.axis_index("slab").astype(F32)
    low = (lax.axis_index("sub") * y_cubes).astype(F32)
    blank = rows[0] != slab + 1.0
    hit = jnp.where(blank, 0.0, 1.0)
    upto = hit
    for step in (1, 2, 4, 8, 16, 32, 64):
        upto = upto + jnp.where(lane >= step, pltpu.roll(upto, step, 1), 0.0)
    result = jnp.zeros(rows[0].shape, F32)
    for slot in range(MOST):
        here = hit * jnp.where(upto == slot + 1.0, 1.0, 0.0)
        for k, cube in enumerate((rows[1] - 1.0 - low, rows[2] - 1.0)):
            first = jnp.sum(here * cube, axis=1, keepdims=True) * EDGE
            result = jnp.where(lane == 2 * slot + k, first, result)
    return result.astype(jnp.int32)


def thirds(value):
    parts = []
    for _ in range(3):
        part = value.astype(BF16)
        parts.append(part)
        value = value - part.astype(F32)
    return parts


def whole_of(rows):
    return jnp.sum(rows.astype(F32), axis=0, keepdims=True)


def coarse_kernel(slabs, xor, cells_shape, *refs):
    _, own, far, x_first, x_second, weight, _ = refs[:7]
    padded, conv, stats, picks, sems = refs[7:]
    dx, dy, dz = cells_shape
    sources = slabs
    asked = [own[dy], x_first[dy], far[dy + 1], far[dy]] if xor else [far[s] for s in range(sources)]
    channels = padded.shape[-1]
    rows = pl.ds(1, dy)
    xa = jnp.where(lax.rem(lax.axis_index("slab"), 2) == 0, dx + 1, 0)
    xb = dx + 1 - xa
    has = inside(xor, slabs)
    first = pltpu.make_async_copy(x_first.at[pl.ds(0, dy)], padded.at[xa, rows], sems.at[0])
    first.start()

    @pl.when(has)
    def _():
        second = pltpu.make_async_copy(x_second.at[pl.ds(0, dy)], padded.at[xb, rows], sems.at[1])
        second.start()
        second.wait()

    @pl.when(jnp.logical_not(has))
    def _():
        padded[xb, rows] = jnp.zeros((dy,) + padded.shape[2:], BF16)

    first.wait()
    means, squares = [], []
    for x in range(dx):
        taken = [
            padded[x + a, pl.ds(b, dy)].reshape(dy * dz, channels)
            for a in range(3)
            for b in range(3)
        ]
        sums = jnp.dot(
            jnp.concatenate(taken, axis=1), wide_weight(weight), preferred_element_type=F32
        )
        value = shifted_sum(sums, dz, channels).reshape(dy, dz, channels)
        conv[x] = value
        if x == 0:
            picks[...] = choose([note.astype(F32) for note in asked], dy // EDGE)
        inner = value[1 : dy - 1].reshape(-1, 8, channels)
        mean = jnp.sum(jnp.sum(inner, axis=0), axis=0, keepdims=True) / ((dy - 2) * dz)
        off = conv[x, pl.ds(1, dy - 2)].reshape(-1, 8, channels) - mean[None]
        means.append(mean)
        squares.append(jnp.sum(jnp.sum(off * off, axis=0), axis=0, keepdims=True))
    mean, square = merge(means, squares, float((dy - 2) * dz))
    stats[0:1, :] = mean
    stats[1:2, :] = square


def edge_kernel(sources, xor, *refs):
    picks, conv_from, stats, y_first, y_second, weight = refs[:6]
    outs = refs[6:-3]
    conv, rim, cube = refs[-3:]
    dx, dy, dz, channels = conv.shape
    slab = lax.axis_index("slab")
    sub = lax.axis_index("sub")
    xa = jnp.where(lax.rem(slab, 2) == 0, dx + 1, 0)
    xb = dx + 1 - xa
    side = jnp.where(lax.rem(sub, 2) == 0, 1, 0)
    for got, place in ((y_first, side), (y_second, 1 - side)):
        rim[place, xa] = got[0]
        rim[place, pl.ds(1, dx)] = got[pl.ds(1, dx)]
        rim[place, xb] = got[dx + 1]
    edges = []
    for place, row, b in ((0, 0, 0), (1, dy - 1, 2)):
        taken = [rim[place, pl.ds(a, dx)].reshape(dx * dz, channels) for a in range(3)]
        taps = jnp.concatenate(
            [
                jnp.concatenate([weight[9 * a + 3 * b + c] for c in range(3)], axis=1)
                for a in range(3)
            ],
            axis=0,
        )
        sums = jnp.dot(jnp.concatenate(taken, axis=1), taps, preferred_element_type=F32)
        value = conv_from[:, row] + shifted_sum(sums, dz, channels).reshape(dx, dz, channels)
        conv[:, row] = value
        edges.append(value.reshape(-1, 8, channels))
    count = 2 * dx * dz
    mean = sum(jnp.sum(jnp.sum(e, axis=0), axis=0, keepdims=True) for e in edges) / count
    square = sum(
        jnp.sum(jnp.sum((e - mean[None]) ** 2, axis=0), axis=0, keepdims=True) for e in edges
    )
    cells = dx * dy * dz
    apart = mean - stats[0:1, :]
    square = square + stats[1:2, :] + apart * apart * (count * (cells - count) / cells)
    mean = stats[0:1, :] + apart * (count / cells)
    tail = jnp.concatenate(thirds(mean) + thirds(square), axis=0).astype(F32)
    tail = jnp.concatenate([tail, jnp.zeros((TAIL - 6, channels), F32)], axis=0).astype(SENT)
    for s in range(sources):
        out = outs[s] if xor else outs[0].at[s]
        for slot in range(MOST):
            first_y = picks[s, 2 * slot]
            first_z = picks[s, 2 * slot + 1]
            for x in range(EDGE):
                for y in range(EDGE):
                    piece = conv[x, first_y + y, pl.ds(first_z, EDGE), :]
                    cube[pl.ds(slot * EDGE**3 + (x * EDGE + y) * EDGE, EDGE), :] = piece
        out[pl.ds(0, MOST * EDGE**3), :] = (cube[...] - mean).astype(SENT)
        out[pl.ds(MOST * EDGE**3, TAIL), :] = tail


def group_sum(value, size):
    lanes = value.shape[-1]
    place = lax.broadcasted_iota(jnp.int32, value.shape, 1) % size
    total = value
    for step in range(1, size):
        total = total + jnp.where(place >= step, pltpu.roll(value, step, 1), 0.0)
        total = total + jnp.where(place + step < size, pltpu.roll(value, lanes - step, 1), 0.0)
    return total


def merge(means, squares, count):
    mean = sum(means) / len(means)
    square = sum(squares)
    for part in means:
        square = square + count * (part - mean) * (part - mean)
    return mean, square


def final_kernel(cube_lists, stat_lists, cells, xor, *refs):
    coords, links = refs[:2]
    cubes = refs[2 : 2 + cube_lists]
    stats = refs[2 + cube_lists : 2 + cube_lists + stat_lists]
    rest = refs[2 + cube_lists + stat_lists :]
    gain, bias, lift, fine, folded = rest[:5]
    pieces, out_to = rest[5:-9], rest[-9]
    held, acted, lifted, twice, frame, spread, out, sems = rest[-8:]
    total, _, channels = fine.shape
    slab = lax.axis_index("slab")
    volume = EDGE**3
    if not xor:
        for slot in range(MOST):
            for s in range(cubes[0].shape[0]):
                held[MOST * s + slot] = cubes[0][s, pl.ds(slot * volume, volume), :].astype(F32) + whole_of(
                    cubes[0][s, pl.ds(MOST * volume, 3), :]
                )
    size = channels // G
    mean, square = merge(
        [s[0:1, :] for s in stats], [s[1:2, :] for s in stats], float(cells)
    )
    cells = cells * stat_lists
    group_mean = group_sum(mean, size) / size
    off = mean - group_mean
    group_var = group_sum(square + cells * off * off, size) / (cells * size)
    scale = lax.rsqrt(group_var + EPS) * gain[...]

    def act(value, n):
        normed = (value - group_mean) * scale + bias[...]
        rows = pl.ds(pl.multiple_of(n * volume, volume), volume)
        acted[rows, :] = (normed / (1.0 + jnp.exp(-normed))).astype(BF16)

    seen = [[jnp.int32(0)] * MOST for _ in cubes]
    for n in range(total):
        holder = coords[0, n]
        rank = jnp.int32(0)
        for m in range(n):
            rank = rank + (coords[0, m] == holder).astype(jnp.int32)
        if xor:
            source = jnp.bitwise_xor(holder, slab)
            for s in range(len(cubes)):
                for slot in range(MOST):
                    here = jnp.logical_and(source == s, rank == slot)
                    seen[s][slot] = jnp.where(here, n, seen[s][slot])
        else:
            act(held[holder * MOST + rank], n)
    if xor:
        for s, cube in enumerate(cubes):
            base = whole_of(cube[pl.ds(MOST * volume, TAIL), :][0:3])
            for slot in range(MOST):
                act(cube[pl.ds(slot * volume, volume), :].astype(F32) + base, seen[s][slot])
    rounded = jnp.dot(acted[...], lift[...], preferred_element_type=F32).astype(BF16).astype(F32)
    rows = total * volume
    twice[pl.ds(0, rows, stride=2), :] = rounded
    twice[pl.ds(1, rows, stride=2), :] = rounded
    flat = EDGE * EDGE
    lifted[...] = rounded.reshape(total, EDGE, flat, channels)
    place = lax.broadcasted_iota(jnp.int32, (flat, channels), 0)
    for n in range(total):
        sides = [neighbour(links, n, direction, total) for direction in range(4)]
        for i in range(-1, EDGE + 1):
            if 0 <= i < EDGE:
                here = lifted[n, i]
                (low, low_on), (high, high_on) = sides[2], sides[3]
                before = jnp.where(low_on, lifted[low, i], 0.0)
                after = jnp.where(high_on, lifted[high, i], 0.0)
                before = pltpu.roll(before, EDGE, 0)
                after = pltpu.roll(after, flat - EDGE, 0)
            else:
                other, on = sides[0] if i < 0 else sides[1]
                here = jnp.where(on, lifted[other, EDGE - 1 if i < 0 else 0], 0.0)
                before = after = jnp.zeros_like(here)
            frame[0, n, i + 1] = jnp.where(
                place < EDGE, before, pltpu.roll(here, EDGE, 0)
            ).astype(BF16)
            frame[1, n, i + 1] = here.astype(BF16)
            frame[2, n, i + 1] = jnp.where(
                place >= flat - EDGE, after, pltpu.roll(here, flat - EDGE, 0)
            ).astype(BF16)
    whole = [piece.at[n] for piece in pieces for n in range(piece.shape[0])]
    step = total // 2
    band = step * volume
    level = lax.broadcasted_iota(jnp.int32, (band, channels), 0) % EDGE
    copies = []
    for first in range(0, total, step):
        for p in range(2):
            for q in range(2):
                taken = [
                    frame[q + b, pl.ds(first, step), pl.ds(p + a, EDGE)].reshape(band, channels)
                    for a in range(2)
                    for b in range(2)
                ]
                sums = jnp.dot(
                    jnp.concatenate(taken, axis=1), folded[2 * p + q], preferred_element_type=F32
                )
                below = pltpu.roll(sums[:, channels : 2 * channels], 1, 0)
                above = pltpu.roll(sums[:, 3 * channels :], band - 1, 0)
                even = sums[:, :channels] + jnp.where(level == 0, 0.0, below)
                odd = sums[:, 2 * channels : 3 * channels] + jnp.where(
                    level == EDGE - 1, 0.0, above
                )
                start = 2 * first * volume
                spread[2 * p + q, pl.ds(start, band, stride=2), :] = even
                spread[2 * p + q, pl.ds(start + 1, band, stride=2), :] = odd
            for n in range(first, first + step):
                for i in range(p, FB, 2):
                    for j in range(0, FB, 2):
                        cell = pl.ds(((n * EDGE + i // 2) * EDGE + j // 2) * FB, FB)
                        pair = pl.ds((i * FB + j) * FB, 2 * FB)
                        up = twice[cell, :]
                        raised = jnp.concatenate([up, up], axis=0)
                        own = (fine[n, pair, :].astype(F32) + raised).astype(BF16).astype(F32)
                        conv = jnp.concatenate(
                            [spread[2 * p, cell, :], spread[2 * p + 1, cell, :]], axis=0
                        )
                        out[n, pair, :] = (own + whole[n][pair, :] + conv).astype(BF16)
                if p:
                    copies.append(pltpu.make_async_copy(out.at[n], out_to.at[n], sems.at[n]))
                    copies[-1].start()
    for copy in copies:
        copy.wait()


SMEM = pl.BlockSpec(memory_space=pltpu.SMEM)
VMEM = pl.BlockSpec(memory_space=pltpu.VMEM)
HBM = pl.BlockSpec(memory_space=pl.ANY)


def limit(mib):
    return pltpu.CompilerParams(vmem_limit_bytes=mib * 2**20)


def fine_part(links, fine, weight, after, first, count, role, coarse_in=None):
    _, cells, channels = fine.shape
    shapes = [jax.ShapeDtypeStruct((count, cells, channels), F32)]
    specs, sems, inputs = [SMEM, VMEM, VMEM, HBM], [], (links, fine, weight, after)
    if role == "load":
        dx, dy, dz, _ = coarse_in.shape
        extra = [fine.shape, weight.shape, (dx + 2, dy + 2, dz, channels)]
        extra.append((4, 4 * channels, 4 * channels))
        shapes += [jax.ShapeDtypeStruct(shape, BF16) for shape in extra]
        hbm = pl.BlockSpec(memory_space=pltpu.HBM)
        specs = [SMEM, hbm, hbm, HBM, hbm]
        sems = [pltpu.SemaphoreType.DMA((3,))]
        fine, weight, coarse_in = (
            pltpu.with_memory_space_constraint(x, pltpu.HBM) for x in (fine, weight, coarse_in)
        )
        inputs = (links, fine, weight, after, coarse_in)
    return pl.pallas_call(
        functools.partial(fine_kernel, first, count, role),
        out_shape=shapes,
        in_specs=specs,
        out_specs=[VMEM] * len(shapes),
        scratch_shapes=[
            pltpu.VMEM((count, FB + 2, FB // 2, 2 * FB, channels), BF16),
            pltpu.VMEM((count, FB + 2, FB // 2 + 1, 2 * FB, channels), BF16),
        ]
        + sems,
        compiler_params=limit(18),
        cost_estimate=pl.CostEstimate(
            flops=2 * 27 * count * cells * channels * channels,
            bytes_accessed=4 * count * cells * channels,
            transcendentals=0,
        ),
        name="fine_part",
    )(*inputs)


def body(
    coarse_in,
    coarse_weight,
    norm_gain,
    norm_bias,
    lift_weight,
    fine_input,
    block_coords,
    neighbours,
    fine_weight,
):
    dx, dy, dz, channels = coarse_in.shape
    slabs, subs = lax.axis_size("slab"), lax.axis_size("sub")
    total = block_coords.shape[0]
    xor = slabs == 4 and total == MOST * slabs
    coords = block_coords.T
    send_a, send_b, row_a, row_b, coords, links = pl.pallas_call(
        send_kernel,
        out_shape=[
            jax.ShapeDtypeStruct((dy + 1, dz, channels), BF16),
            jax.ShapeDtypeStruct((dy + 2, dz, channels), BF16),
            jax.ShapeDtypeStruct((dx, dz, channels), BF16),
            jax.ShapeDtypeStruct((dx, dz, channels), BF16),
            jax.ShapeDtypeStruct(coords.shape, jnp.int32),
            jax.ShapeDtypeStruct(neighbours.shape, jnp.int32),
        ],
        in_specs=[pl.BlockSpec(memory_space=pltpu.HBM)] * 3,
        out_specs=[VMEM] * 6,
        scratch_shapes=[pltpu.VMEM((dz, channels), jnp.int32), pltpu.SemaphoreType.DMA((6,))],
        compiler_params=limit(4),
        name="send",
    )(*(pltpu.with_memory_space_constraint(x, pltpu.HBM) for x in (coarse_in, coords, neighbours)))
    x_first = lax.ppermute(send_a, "slab", pairs(slabs, 0))
    if xor:
        send_b = pl.pallas_call(
            relay_kernel,
            out_shape=jax.ShapeDtypeStruct(send_b.shape, BF16),
            in_specs=[VMEM] * 2,
            out_specs=VMEM,
            input_output_aliases={1: 0},
            compiler_params=limit(4),
            name="relay",
        )(x_first, send_b)
        far = x_second = lax.ppermute(send_b, "slab", xor_links(slabs, 3))
    else:
        x_second = lax.ppermute(send_b, "slab", pairs(slabs, 1))
        far = lax.all_gather(send_a[dy], "slab", axis=0)
    shares = [0, total * 3 // 8, total * 3 // 4, total]
    pieces = []

    def fill(index, after, waiting, role="plain"):
        begin = shares[index]
        count = shares[index + 1] - begin
        made = fine_part(links, fine, weight, after, begin, count, role, coarse_in)
        made, waiting = lax.optimization_barrier((made, waiting))
        pieces.append(made[0])
        return made[1:], waiting

    fine, weight = fine_input, fine_weight
    made, x_second = fill(0, send_b, x_second, "load")
    if xor:
        far = x_second
    fine, weight, padded, folded = made
    line_a, line_b = pl.pallas_call(
        functools.partial(line_kernel, slabs, xor),
        out_shape=[jax.ShapeDtypeStruct((dx + 2, dz, channels), BF16)] * 2,
        in_specs=[VMEM] * 4,
        out_specs=[VMEM] * 2,
        compiler_params=limit(4),
        name="line",
    )(x_first, x_second, row_a, row_b)
    y_first = lax.ppermute(line_a, "sub", pairs(subs, 0))
    y_second = lax.ppermute(line_b, "sub", pairs(subs, 1))

    padded, conv, stats, picks = pl.pallas_call(
        functools.partial(coarse_kernel, slabs, xor, (dx, dy, dz)),
        out_shape=[
            jax.ShapeDtypeStruct(padded.shape, BF16),
            jax.ShapeDtypeStruct(coarse_in.shape, F32),
            jax.ShapeDtypeStruct((8, channels), F32),
            jax.ShapeDtypeStruct((slabs, channels), jnp.int32),
        ],
        in_specs=[VMEM] * 6 + [HBM],
        out_specs=[VMEM] * 4,
        scratch_shapes=[pltpu.SemaphoreType.DMA((2,))],
        input_output_aliases={0: 0},
        compiler_params=limit(12),
        cost_estimate=pl.CostEstimate(
            flops=2 * 27 * dx * dy * dz * channels * channels,
            bytes_accessed=4 * dx * dy * dz * channels,
            transcendentals=0,
        ),
        name="coarse",
    )(padded, send_a, far, x_first, x_second, coarse_weight, line_a)
    (conv, stats), (y_first, y_second) = lax.optimization_barrier(
        ((conv, stats), (y_first, y_second))
    )
    piece = (MOST * EDGE**3 + TAIL, channels)
    if xor:
        shapes = [jax.ShapeDtypeStruct(piece, SENT)] * slabs
    else:
        shapes = [jax.ShapeDtypeStruct((slabs,) + piece, SENT)]
    results = pl.pallas_call(
        functools.partial(edge_kernel, slabs, xor),
        out_shape=shapes + [jax.ShapeDtypeStruct(conv.shape, F32)],
        in_specs=[SMEM] + [VMEM] * 5,
        out_specs=[VMEM] * (len(shapes) + 1),
        scratch_shapes=[
            pltpu.VMEM((2, dx + 2, dz, channels), BF16),
            pltpu.VMEM((MOST * EDGE**3, channels), F32),
        ],
        input_output_aliases={1: len(shapes)},
        compiler_params=limit(8),
        name="edge",
    )(picks, conv, stats, y_first, y_second, coarse_weight)
    sent = results[:-1]
    cells = dx * dy * dz
    row = MOST * EDGE**3
    if xor:
        replies = [sent[0]] + [
            lax.ppermute(sent[distance], "slab", xor_links(slabs, distance))
            for distance in range(1, slabs)
        ]
        parts = [r[row : row + 6] for r in replies]
    else:
        replies = [lax.all_to_all(sent[0], "slab", split_axis=0, concat_axis=0, tiled=True)]
        parts = [replies[0][s, row : row + 6] for s in range(slabs)]
    _, parts = fill(1, sent[0], parts)
    mean, square = merge([whole_of(p[0:3]) for p in parts], [whole_of(p[3:6]) for p in parts], float(cells))
    cells = cells * slabs
    merged = jnp.concatenate([mean, square])
    if subs == 4:
        lines = [merged] + [
            lax.ppermute(merged, "sub", xor_links(subs, distance)) for distance in range(1, subs)
        ]
    else:
        lines = list(lax.all_gather(merged, "sub", axis=0))
    _, lines = fill(2, merged, lines)

    volume = EDGE**3
    return pl.pallas_call(
        functools.partial(final_kernel, len(replies), len(lines), cells, xor),
        out_shape=jax.ShapeDtypeStruct(fine_input.shape, BF16),
        in_specs=[SMEM] * 2 + [VMEM] * (len(replies) + len(lines) + 5 + len(pieces)),
        out_specs=HBM,
        scratch_shapes=[
            pltpu.VMEM((slabs * MOST, volume, channels), F32),
            pltpu.VMEM((total * volume, channels), BF16),
            pltpu.VMEM((total, EDGE, EDGE * EDGE, channels), F32),
            pltpu.VMEM((2 * total * volume, channels), F32),
            pltpu.VMEM((3, total, EDGE + 2, EDGE * EDGE, channels), BF16),
            pltpu.VMEM((4, 2 * total * volume, channels), F32),
            pltpu.VMEM(fine_input.shape, BF16),
            pltpu.SemaphoreType.DMA((total,)),
        ],
        compiler_params=limit(18),
        name="final",
    )(
        coords,
        links,
        *replies,
        *lines,
        norm_gain.reshape(1, channels),
        norm_bias.reshape(1, channels),
        lift_weight,
        fine,
        folded,
        *pieces,
    )


def solution(mesh):
    in_specs = (
        P(("scene", "slab"), "sub", None, None),
        P(),
        P(),
        P(),
        P(),
        P(("scene", "slab", "sub"), None, None),
        P(("scene", "slab", "sub"), None),
        P(("scene", "slab", "sub"), None),
        P(),
    )
    out_specs = P(("scene", "slab", "sub"), None, None)
    return jax.shard_map(body, mesh=mesh, in_specs=in_specs, out_specs=out_specs, check_vma=False)
```

```python
import functools

import jax
import jax.numpy as jnp
from jax import lax
from jax.experimental import pallas as pl
from jax.experimental.pallas import tpu as pltpu
from jax.sharding import PartitionSpec as P


G = 32
FB = 8
EDGE = FB // 2
MOST = 2
TAIL = 16
SENT = jnp.bfloat16
EPS = 1e-05
F32 = jnp.float32
BF16 = jnp.bfloat16


def pairs(count, odd):
    links = []
    for i in range(odd, count - 1, 2):
        links += [(i, i + 1), (i + 1, i)]
    return links


def xor_links(count, distance):
    return [(i, i ^ distance) for i in range(count)]


def shifted_sum(sums, depth, channels):
    rows = sums.shape[0]
    place = lax.broadcasted_iota(jnp.int32, (rows, channels), 0) % depth
    below = pltpu.roll(sums[:, :channels], 1, 0)
    above = pltpu.roll(sums[:, 2 * channels :], rows - 1, 0)
    return (
        sums[:, channels : 2 * channels]
        + jnp.where(place == 0, 0.0, below)
        + jnp.where(place == depth - 1, 0.0, above)
    )


def convolved(get, weight, outer, depth):
    channels = weight.shape[1]
    taken = jnp.concatenate(
        [
            jnp.concatenate([get(i + a, b) for i in range(outer)], axis=0)
            for a in range(3)
            for b in range(3)
        ],
        axis=1,
    )
    taps = jnp.concatenate(
        [jnp.concatenate([weight[3 * ab], weight[3 * ab + 1]], axis=1) for ab in range(9)], axis=0
    )
    sums = jnp.dot(taken, taps, preferred_element_type=F32)
    zero = jnp.zeros((channels, channels), BF16)
    taken = jnp.concatenate(
        [
            jnp.concatenate([get(i + a, b) for i in range(0, outer, 2)], axis=0)
            for a in range(4)
            for b in range(3)
        ],
        axis=1,
    )
    taps = jnp.concatenate(
        [
            jnp.concatenate(
                [
                    weight[3 * (3 * a + b) + 2] if a < 3 else zero,
                    weight[3 * (3 * a - 3 + b) + 2] if a else zero,
                ],
                axis=1,
            )
            for a in range(4)
            for b in range(3)
        ],
        axis=0,
    )
    above = jnp.dot(taken, taps, preferred_element_type=F32)
    rows = sums.shape[0]
    plane = rows // outer
    above = jnp.concatenate(
        [
            above[i // 2 * plane : (i // 2 + 1) * plane, i % 2 * channels : (i % 2 + 1) * channels]
            for i in range(outer)
        ],
        axis=0,
    )
    place = lax.broadcasted_iota(jnp.int32, (rows, channels), 0) % depth
    return (
        sums[:, channels:]
        + jnp.where(place == 0, 0.0, pltpu.roll(sums[:, :channels], 1, 0))
        + jnp.where(place == depth - 1, 0.0, pltpu.roll(above, rows - 1, 0))
    )


def neighbour(links, n, direction, total):
    target = links[n, direction]
    return lax.rem(jnp.maximum(target, 0), total), target >= 0


def fold_weights(weight, out):
    channels = weight.shape[1]
    taps = (((0,), (1, 2)), ((0, 1), (2,)))
    for p in range(2):
        for q in range(2):
            for a in range(2):
                for b in range(2):
                    sums = []
                    for c in range(3):
                        parts = [
                            weight[9 * i + 3 * j + c].astype(F32)
                            for i in taps[p][a]
                            for j in taps[q][b]
                        ]
                        sums.append(functools.reduce(jnp.add, parts))
                    kinds = [sums[1] + sums[2], sums[0], sums[0] + sums[1], sums[2]]
                    rows = pl.ds((2 * a + b) * channels, channels)
                    for k, kind in enumerate(kinds):
                        out[2 * p + q, rows, pl.ds(k * channels, channels)] = kind.astype(BF16)


def parity(name, length):
    return jnp.where(lax.rem(lax.axis_index(name), 2) == 0, length - 1, 0)


def send_kernel(inp, coords, links, send_a, send_b, row_a, row_b, coords_out, links_out, note, sems):
    dx, dy = inp.shape[:2]
    xa, ya = parity("slab", dx), parity("sub", dy)
    moves = [
        (coords, coords_out),
        (inp.at[xa], send_a.at[pl.ds(0, dy)]),
        (inp.at[dx - 1 - xa], send_b.at[pl.ds(0, dy)]),
        (inp.at[:, ya], row_a),
        (inp.at[:, dy - 1 - ya], row_b),
        (links, links_out),
    ]
    copies = [pltpu.make_async_copy(a, b, sems.at[i]) for i, (a, b) in enumerate(moves)]
    for copy in copies:
        copy.start()
    note[...] = jnp.zeros_like(note)
    copies[0].wait()
    note[pl.ds(0, coords.shape[0]), pl.ds(0, coords.shape[1])] = coords_out[...] + 1
    send_a[dy] = note[...].astype(F32).astype(BF16)
    send_b[dy] = send_a[dy]
    send_b[dy + 1] = jnp.zeros_like(send_a[dy])
    for copy in copies[1:]:
        copy.wait()


def relay_kernel(x_first, _, send_b):
    send_b[send_b.shape[0] - 1] = x_first[x_first.shape[0] - 1]


def inside(xor, slabs):
    slab = lax.axis_index("slab")
    return jnp.logical_or(not xor, jnp.logical_and(slab > 0, slab < slabs - 1))


def line_kernel(slabs, xor, x_first, x_second, row_a, row_b, line_a, line_b):
    dx, dy = row_a.shape[0], x_first.shape[0] - 1
    has = inside(xor, slabs)
    ya = parity("sub", dy)
    for place, row, line in ((ya, row_a, line_a), (dy - 1 - ya, row_b, line_b)):
        line[0] = x_first[place]
        line[pl.ds(1, dx)] = row[...]
        line[dx + 1] = jnp.where(has, x_second[place], jnp.zeros_like(x_second[place]))


def fine_kernel(first, count, role, *refs):
    loads = []
    if role == "load":
        links, fine_from, weight_from, _, inp = refs[:5]
        out, fine, weight, padded, folded, even, odd, sems = refs[5:]
        dx, dy = inp.shape[:2]
        moves = [
            (fine_from, fine),
            (weight_from, weight),
            (inp, padded.at[pl.ds(1, dx), pl.ds(1, dy)]),
        ]
        loads = [pltpu.make_async_copy(a, b, sems.at[i]) for i, (a, b) in enumerate(moves)]
        for load in loads:
            load.start()
        for y in (0, dy + 1):
            padded[:, y] = jnp.zeros((dx + 2,) + padded.shape[2:], BF16)
        loads[0].wait()
    else:
        links, fine, weight, _, out, even, odd = refs
    total, _, channels = fine.shape
    tile = 2 * FB
    lines = FB // 2

    def plane(n, i):
        return fine[n, pl.ds(i * FB * FB, FB * FB), :].reshape(lines, tile, channels)

    zero = jnp.zeros((FB, channels), F32)
    for slot in range(count):
        n = first + slot
        sides = [neighbour(links, n, direction, total) for direction in range(4)]
        for i in range(-1, FB + 1):
            if 0 <= i < FB:
                here = plane(n, i)
                (low, low_on), (high, high_on) = sides[2], sides[3]
                before = fine[low, pl.ds(i * FB * FB + FB * FB - tile, tile), :].astype(F32)
                after = fine[high, pl.ds(i * FB * FB, tile), :].astype(F32)
                before = jnp.where(low_on, before[FB:], 0.0)
                after = jnp.where(high_on, after[:FB], 0.0)
            else:
                other, on = sides[0] if i < 0 else sides[1]
                here = plane(other, FB - 1 if i < 0 else 0)
                here = jnp.where(on, here, jnp.zeros_like(here))
                before = after = zero
            even[slot, i + 1] = here
            wide = here.astype(F32)
            halves = [before]
            for line in range(lines):
                halves += [wide[line, :FB], wide[line, FB:]]
            halves.append(after)
            for line in range(lines + 1):
                odd[slot, i + 1, line] = jnp.concatenate(
                    halves[2 * line : 2 * line + 2], axis=0
                ).astype(BF16)
        if role == "load" and slot == 0:
            loads[1].wait()

        def get(plane_index, b, slot=slot):
            if b == 1:
                part = even[slot, plane_index]
            else:
                part = odd[slot, plane_index, pl.ds(b // 2, lines)]
            return part.reshape(FB * FB, channels)

        out[slot] = convolved(get, weight, FB, FB)
    if role == "load":
        fold_weights(weight, folded)
    for load in loads[2:]:
        load.wait()


def choose(notes, y_cubes):
    rows = [jnp.concatenate([note[k : k + 1] for note in notes], axis=0) for k in range(3)]
    lane = lax.broadcasted_iota(jnp.int32, rows[0].shape, 1)
    slab = lax.axis_index("slab").astype(F32)
    low = (lax.axis_index("sub") * y_cubes).astype(F32)
    blank = rows[0] != slab + 1.0
    hit = jnp.where(blank, 0.0, 1.0)
    upto = hit
    for step in (1, 2, 4, 8, 16, 32, 64):
        upto = upto + jnp.where(lane >= step, pltpu.roll(upto, step, 1), 0.0)
    result = jnp.zeros(rows[0].shape, F32)
    for slot in range(MOST):
        here = hit * jnp.where(upto == slot + 1.0, 1.0, 0.0)
        for k, cube in enumerate((rows[1] - 1.0 - low, rows[2] - 1.0)):
            first = jnp.sum(here * cube, axis=1, keepdims=True) * EDGE
            result = jnp.where(lane == 2 * slot + k, first, result)
    return result.astype(jnp.int32)


def thirds(value):
    parts = []
    for _ in range(3):
        part = value.astype(BF16)
        parts.append(part)
        value = value - part.astype(F32)
    return parts


def whole_of(rows):
    return jnp.sum(rows.astype(F32), axis=0, keepdims=True)


def coarse_kernel(slabs, xor, cells_shape, *refs):
    _, own, far, x_first, x_second, weight, _ = refs[:7]
    padded, conv, stats, picks, sems = refs[7:]
    dx, dy, dz = cells_shape
    sources = slabs
    asked = [own[dy], x_first[dy], far[dy + 1], far[dy]] if xor else [far[s] for s in range(sources)]
    channels = padded.shape[-1]
    rows = pl.ds(1, dy)
    xa = jnp.where(lax.rem(lax.axis_index("slab"), 2) == 0, dx + 1, 0)
    xb = dx + 1 - xa
    has = inside(xor, slabs)
    first = pltpu.make_async_copy(x_first.at[pl.ds(0, dy)], padded.at[xa, rows], sems.at[0])
    first.start()

    @pl.when(has)
    def _():
        second = pltpu.make_async_copy(x_second.at[pl.ds(0, dy)], padded.at[xb, rows], sems.at[1])
        second.start()
        second.wait()

    @pl.when(jnp.logical_not(has))
    def _():
        padded[xb, rows] = jnp.zeros((dy,) + padded.shape[2:], BF16)

    first.wait()
    means, squares = [], []
    for x in range(dx):
        if x % 2 == 0:

            def get(plane_index, b, x=x):
                return padded[x + plane_index, pl.ds(b, dy)].reshape(dy * dz, channels)

            both = convolved(get, weight, 2, dz).reshape(2, dy, dz, channels)
        value = both[x % 2]
        conv[x] = value
        if x == 0:
            picks[...] = choose([note.astype(F32) for note in asked], dy // EDGE)
        inner = value[1 : dy - 1].reshape(-1, 8, channels)
        mean = jnp.sum(jnp.sum(inner, axis=0), axis=0, keepdims=True) / ((dy - 2) * dz)
        off = conv[x, pl.ds(1, dy - 2)].reshape(-1, 8, channels) - mean[None]
        means.append(mean)
        squares.append(jnp.sum(jnp.sum(off * off, axis=0), axis=0, keepdims=True))
    mean, square = merge(means, squares, float((dy - 2) * dz))
    stats[0:1, :] = mean
    stats[1:2, :] = square


def edge_kernel(sources, xor, *refs):
    picks, conv_from, stats, y_first, y_second, weight = refs[:6]
    outs = refs[6:-3]
    conv, rim, cube = refs[-3:]
    dx, dy, dz, channels = conv.shape
    slab = lax.axis_index("slab")
    sub = lax.axis_index("sub")
    xa = jnp.where(lax.rem(slab, 2) == 0, dx + 1, 0)
    xb = dx + 1 - xa
    side = jnp.where(lax.rem(sub, 2) == 0, 1, 0)
    for got, place in ((y_first, side), (y_second, 1 - side)):
        rim[place, xa] = got[0]
        rim[place, pl.ds(1, dx)] = got[pl.ds(1, dx)]
        rim[place, xb] = got[dx + 1]
    edges = []
    for place, row, b in ((0, 0, 0), (1, dy - 1, 2)):
        taken = [rim[place, pl.ds(a, dx)].reshape(dx * dz, channels) for a in range(3)]
        taps = jnp.concatenate(
            [
                jnp.concatenate([weight[9 * a + 3 * b + c] for c in range(3)], axis=1)
                for a in range(3)
            ],
            axis=0,
        )
        sums = jnp.dot(jnp.concatenate(taken, axis=1), taps, preferred_element_type=F32)
        value = conv_from[:, row] + shifted_sum(sums, dz, channels).reshape(dx, dz, channels)
        conv[:, row] = value
        edges.append(value.reshape(-1, 8, channels))
    count = 2 * dx * dz
    mean = sum(jnp.sum(jnp.sum(e, axis=0), axis=0, keepdims=True) for e in edges) / count
    square = sum(
        jnp.sum(jnp.sum((e - mean[None]) ** 2, axis=0), axis=0, keepdims=True) for e in edges
    )
    cells = dx * dy * dz
    apart = mean - stats[0:1, :]
    square = square + stats[1:2, :] + apart * apart * (count * (cells - count) / cells)
    mean = stats[0:1, :] + apart * (count / cells)
    tail = jnp.concatenate(thirds(mean) + thirds(square), axis=0).astype(F32)
    tail = jnp.concatenate([tail, jnp.zeros((TAIL - 6, channels), F32)], axis=0).astype(SENT)
    for s in range(sources):
        out = outs[s] if xor else outs[0].at[s]
        for slot in range(MOST):
            first_y = picks[s, 2 * slot]
            first_z = picks[s, 2 * slot + 1]
            for x in range(EDGE):
                for y in range(EDGE):
                    piece = conv[x, first_y + y, pl.ds(first_z, EDGE), :]
                    cube[pl.ds(slot * EDGE**3 + (x * EDGE + y) * EDGE, EDGE), :] = piece
        out[pl.ds(0, MOST * EDGE**3), :] = (cube[...] - mean).astype(SENT)
        out[pl.ds(MOST * EDGE**3, TAIL), :] = tail


def group_sum(value, size):
    lanes = value.shape[-1]
    place = lax.broadcasted_iota(jnp.int32, value.shape, 1) % size
    total = value
    for step in range(1, size):
        total = total + jnp.where(place >= step, pltpu.roll(value, step, 1), 0.0)
        total = total + jnp.where(place + step < size, pltpu.roll(value, lanes - step, 1), 0.0)
    return total


def merge(means, squares, count):
    mean = sum(means) / len(means)
    square = sum(squares)
    for part in means:
        square = square + count * (part - mean) * (part - mean)
    return mean, square


def final_kernel(cube_lists, stat_lists, cells, xor, *refs):
    coords, links = refs[:2]
    cubes = refs[2 : 2 + cube_lists]
    stats = refs[2 + cube_lists : 2 + cube_lists + stat_lists]
    rest = refs[2 + cube_lists + stat_lists :]
    gain, bias, lift, fine, folded = rest[:5]
    pieces, out_to = rest[5:-9], rest[-9]
    held, acted, lifted, twice, frame, spread, out, sems = rest[-8:]
    total, _, channels = fine.shape
    slab = lax.axis_index("slab")
    volume = EDGE**3
    if not xor:
        for slot in range(MOST):
            for s in range(cubes[0].shape[0]):
                held[MOST * s + slot] = cubes[0][s, pl.ds(slot * volume, volume), :].astype(F32) + whole_of(
                    cubes[0][s, pl.ds(MOST * volume, 3), :]
                )
    size = channels // G
    mean, square = merge(
        [s[0:1, :] for s in stats], [s[1:2, :] for s in stats], float(cells)
    )
    cells = cells * stat_lists
    group_mean = group_sum(mean, size) / size
    off = mean - group_mean
    group_var = group_sum(square + cells * off * off, size) / (cells * size)
    scale = lax.rsqrt(group_var + EPS) * gain[...]

    def act(value, n):
        normed = (value - group_mean) * scale + bias[...]
        rows = pl.ds(pl.multiple_of(n * volume, volume), volume)
        acted[rows, :] = (normed / (1.0 + jnp.exp(-normed))).astype(BF16)

    seen = [[jnp.int32(0)] * MOST for _ in cubes]
    for n in range(total):
        holder = coords[0, n]
        rank = jnp.int32(0)
        for m in range(n):
            rank = rank + (coords[0, m] == holder).astype(jnp.int32)
        if xor:
            source = jnp.bitwise_xor(holder, slab)
            for s in range(len(cubes)):
                for slot in range(MOST):
                    here = jnp.logical_and(source == s, rank == slot)
                    seen[s][slot] = jnp.where(here, n, seen[s][slot])
        else:
            act(held[holder * MOST + rank], n)
    if xor:
        for s, cube in enumerate(cubes):
            base = whole_of(cube[pl.ds(MOST * volume, TAIL), :][0:3])
            for slot in range(MOST):
                act(cube[pl.ds(slot * volume, volume), :].astype(F32) + base, seen[s][slot])
    rounded = jnp.dot(acted[...], lift[...], preferred_element_type=F32).astype(BF16).astype(F32)
    rows = total * volume
    twice[pl.ds(0, rows, stride=2), :] = rounded
    twice[pl.ds(1, rows, stride=2), :] = rounded
    flat = EDGE * EDGE
    lifted[...] = rounded.reshape(total, EDGE, flat, channels)
    place = lax.broadcasted_iota(jnp.int32, (flat, channels), 0)
    for n in range(total):
        sides = [neighbour(links, n, direction, total) for direction in range(4)]
        for i in range(-1, EDGE + 1):
            if 0 <= i < EDGE:
                here = lifted[n, i]
                (low, low_on), (high, high_on) = sides[2], sides[3]
                before = jnp.where(low_on, lifted[low, i], 0.0)
                after = jnp.where(high_on, lifted[high, i], 0.0)
                before = pltpu.roll(before, EDGE, 0)
                after = pltpu.roll(after, flat - EDGE, 0)
            else:
                other, on = sides[0] if i < 0 else sides[1]
                here = jnp.where(on, lifted[other, EDGE - 1 if i < 0 else 0], 0.0)
                before = after = jnp.zeros_like(here)
            frame[0, n, i + 1] = jnp.where(
                place < EDGE, before, pltpu.roll(here, EDGE, 0)
            ).astype(BF16)
            frame[1, n, i + 1] = here.astype(BF16)
            frame[2, n, i + 1] = jnp.where(
                place >= flat - EDGE, after, pltpu.roll(here, flat - EDGE, 0)
            ).astype(BF16)
    whole = [piece.at[n] for piece in pieces for n in range(piece.shape[0])]
    step = total // 2
    band = step * volume
    level = lax.broadcasted_iota(jnp.int32, (band, channels), 0) % EDGE
    copies = []
    for first in range(0, total, step):
        for p in range(2):
            for q in range(2):
                taken = [
                    frame[q + b, pl.ds(first, step), pl.ds(p + a, EDGE)].reshape(band, channels)
                    for a in range(2)
                    for b in range(2)
                ]
                sums = jnp.dot(
                    jnp.concatenate(taken, axis=1), folded[2 * p + q], preferred_element_type=F32
                )
                below = pltpu.roll(sums[:, channels : 2 * channels], 1, 0)
                above = pltpu.roll(sums[:, 3 * channels :], band - 1, 0)
                even = sums[:, :channels] + jnp.where(level == 0, 0.0, below)
                odd = sums[:, 2 * channels : 3 * channels] + jnp.where(
                    level == EDGE - 1, 0.0, above
                )
                start = 2 * first * volume
                spread[2 * p + q, pl.ds(start, band, stride=2), :] = even
                spread[2 * p + q, pl.ds(start + 1, band, stride=2), :] = odd
            for n in range(first, first + step):
                for i in range(p, FB, 2):
                    for j in range(0, FB, 2):
                        cell = pl.ds(((n * EDGE + i // 2) * EDGE + j // 2) * FB, FB)
                        pair = pl.ds((i * FB + j) * FB, 2 * FB)
                        up = twice[cell, :]
                        raised = jnp.concatenate([up, up], axis=0)
                        own = (fine[n, pair, :].astype(F32) + raised).astype(BF16).astype(F32)
                        conv = jnp.concatenate(
                            [spread[2 * p, cell, :], spread[2 * p + 1, cell, :]], axis=0
                        )
                        out[n, pair, :] = (own + whole[n][pair, :] + conv).astype(BF16)
                if p:
                    copies.append(pltpu.make_async_copy(out.at[n], out_to.at[n], sems.at[n]))
                    copies[-1].start()
    for copy in copies:
        copy.wait()


SMEM = pl.BlockSpec(memory_space=pltpu.SMEM)
VMEM = pl.BlockSpec(memory_space=pltpu.VMEM)
HBM = pl.BlockSpec(memory_space=pl.ANY)


def limit(mib):
    return pltpu.CompilerParams(vmem_limit_bytes=mib * 2**20)


def fine_part(links, fine, weight, after, first, count, role, coarse_in=None):
    _, cells, channels = fine.shape
    shapes = [jax.ShapeDtypeStruct((count, cells, channels), F32)]
    specs, sems, inputs = [SMEM, VMEM, VMEM, HBM], [], (links, fine, weight, after)
    if role == "load":
        dx, dy, dz, _ = coarse_in.shape
        extra = [fine.shape, weight.shape, (dx + 2, dy + 2, dz, channels)]
        extra.append((4, 4 * channels, 4 * channels))
        shapes += [jax.ShapeDtypeStruct(shape, BF16) for shape in extra]
        hbm = pl.BlockSpec(memory_space=pltpu.HBM)
        specs = [SMEM, hbm, hbm, HBM, hbm]
        sems = [pltpu.SemaphoreType.DMA((3,))]
        fine, weight, coarse_in = (
            pltpu.with_memory_space_constraint(x, pltpu.HBM) for x in (fine, weight, coarse_in)
        )
        inputs = (links, fine, weight, after, coarse_in)
    return pl.pallas_call(
        functools.partial(fine_kernel, first, count, role),
        out_shape=shapes,
        in_specs=specs,
        out_specs=[VMEM] * len(shapes),
        scratch_shapes=[
            pltpu.VMEM((count, FB + 2, FB // 2, 2 * FB, channels), BF16),
            pltpu.VMEM((count, FB + 2, FB // 2 + 1, 2 * FB, channels), BF16),
        ]
        + sems,
        compiler_params=limit(18),
        cost_estimate=pl.CostEstimate(
            flops=2 * 27 * count * cells * channels * channels,
            bytes_accessed=4 * count * cells * channels,
            transcendentals=0,
        ),
        name="fine_part",
    )(*inputs)


def body(
    coarse_in,
    coarse_weight,
    norm_gain,
    norm_bias,
    lift_weight,
    fine_input,
    block_coords,
    neighbours,
    fine_weight,
):
    dx, dy, dz, channels = coarse_in.shape
    slabs, subs = lax.axis_size("slab"), lax.axis_size("sub")
    total = block_coords.shape[0]
    xor = slabs == 4 and total == MOST * slabs
    coords = block_coords.T
    send_a, send_b, row_a, row_b, coords, links = pl.pallas_call(
        send_kernel,
        out_shape=[
            jax.ShapeDtypeStruct((dy + 1, dz, channels), BF16),
            jax.ShapeDtypeStruct((dy + 2, dz, channels), BF16),
            jax.ShapeDtypeStruct((dx, dz, channels), BF16),
            jax.ShapeDtypeStruct((dx, dz, channels), BF16),
            jax.ShapeDtypeStruct(coords.shape, jnp.int32),
            jax.ShapeDtypeStruct(neighbours.shape, jnp.int32),
        ],
        in_specs=[pl.BlockSpec(memory_space=pltpu.HBM)] * 3,
        out_specs=[VMEM] * 6,
        scratch_shapes=[pltpu.VMEM((dz, channels), jnp.int32), pltpu.SemaphoreType.DMA((6,))],
        compiler_params=limit(4),
        name="send",
    )(*(pltpu.with_memory_space_constraint(x, pltpu.HBM) for x in (coarse_in, coords, neighbours)))
    x_first = lax.ppermute(send_a, "slab", pairs(slabs, 0))
    if xor:
        send_b = pl.pallas_call(
            relay_kernel,
            out_shape=jax.ShapeDtypeStruct(send_b.shape, BF16),
            in_specs=[VMEM] * 2,
            out_specs=VMEM,
            input_output_aliases={1: 0},
            compiler_params=limit(4),
            name="relay",
        )(x_first, send_b)
        far = x_second = lax.ppermute(send_b, "slab", xor_links(slabs, 3))
    else:
        x_second = lax.ppermute(send_b, "slab", pairs(slabs, 1))
        far = lax.all_gather(send_a[dy], "slab", axis=0)
    shares = [0, total * 3 // 8, total * 3 // 4, total]
    pieces = []

    def fill(index, after, waiting, role="plain"):
        begin = shares[index]
        count = shares[index + 1] - begin
        made = fine_part(links, fine, weight, after, begin, count, role, coarse_in)
        made, waiting = lax.optimization_barrier((made, waiting))
        pieces.append(made[0])
        return made[1:], waiting

    fine, weight = fine_input, fine_weight
    made, x_second = fill(0, send_b, x_second, "load")
    if xor:
        far = x_second
    fine, weight, padded, folded = made
    line_a, line_b = pl.pallas_call(
        functools.partial(line_kernel, slabs, xor),
        out_shape=[jax.ShapeDtypeStruct((dx + 2, dz, channels), BF16)] * 2,
        in_specs=[VMEM] * 4,
        out_specs=[VMEM] * 2,
        compiler_params=limit(4),
        name="line",
    )(x_first, x_second, row_a, row_b)
    y_first = lax.ppermute(line_a, "sub", pairs(subs, 0))
    y_second = lax.ppermute(line_b, "sub", pairs(subs, 1))

    padded, conv, stats, picks = pl.pallas_call(
        functools.partial(coarse_kernel, slabs, xor, (dx, dy, dz)),
        out_shape=[
            jax.ShapeDtypeStruct(padded.shape, BF16),
            jax.ShapeDtypeStruct(coarse_in.shape, F32),
            jax.ShapeDtypeStruct((8, channels), F32),
            jax.ShapeDtypeStruct((slabs, channels), jnp.int32),
        ],
        in_specs=[VMEM] * 6 + [HBM],
        out_specs=[VMEM] * 4,
        scratch_shapes=[pltpu.SemaphoreType.DMA((2,))],
        input_output_aliases={0: 0},
        compiler_params=limit(12),
        cost_estimate=pl.CostEstimate(
            flops=2 * 27 * dx * dy * dz * channels * channels,
            bytes_accessed=4 * dx * dy * dz * channels,
            transcendentals=0,
        ),
        name="coarse",
    )(padded, send_a, far, x_first, x_second, coarse_weight, line_a)
    (conv, stats), (y_first, y_second) = lax.optimization_barrier(
        ((conv, stats), (y_first, y_second))
    )
    piece = (MOST * EDGE**3 + TAIL, channels)
    if xor:
        shapes = [jax.ShapeDtypeStruct(piece, SENT)] * slabs
    else:
        shapes = [jax.ShapeDtypeStruct((slabs,) + piece, SENT)]
    results = pl.pallas_call(
        functools.partial(edge_kernel, slabs, xor),
        out_shape=shapes + [jax.ShapeDtypeStruct(conv.shape, F32)],
        in_specs=[SMEM] + [VMEM] * 5,
        out_specs=[VMEM] * (len(shapes) + 1),
        scratch_shapes=[
            pltpu.VMEM((2, dx + 2, dz, channels), BF16),
            pltpu.VMEM((MOST * EDGE**3, channels), F32),
        ],
        input_output_aliases={1: len(shapes)},
        compiler_params=limit(8),
        name="edge",
    )(picks, conv, stats, y_first, y_second, coarse_weight)
    sent = results[:-1]
    cells = dx * dy * dz
    row = MOST * EDGE**3
    if xor:
        replies = [sent[0]] + [
            lax.ppermute(sent[distance], "slab", xor_links(slabs, distance))
            for distance in range(1, slabs)
        ]
        parts = [r[row : row + 6] for r in replies]
    else:
        replies = [lax.all_to_all(sent[0], "slab", split_axis=0, concat_axis=0, tiled=True)]
        parts = [replies[0][s, row : row + 6] for s in range(slabs)]
    _, parts = fill(1, sent[0], parts)
    mean, square = merge([whole_of(p[0:3]) for p in parts], [whole_of(p[3:6]) for p in parts], float(cells))
    cells = cells * slabs
    merged = jnp.concatenate([mean, square])
    if subs == 4:
        lines = [merged] + [
            lax.ppermute(merged, "sub", xor_links(subs, distance)) for distance in range(1, subs)
        ]
    else:
        lines = list(lax.all_gather(merged, "sub", axis=0))
    _, lines = fill(2, merged, lines)

    volume = EDGE**3
    return pl.pallas_call(
        functools.partial(final_kernel, len(replies), len(lines), cells, xor),
        out_shape=jax.ShapeDtypeStruct(fine_input.shape, BF16),
        in_specs=[SMEM] * 2 + [VMEM] * (len(replies) + len(lines) + 5 + len(pieces)),
        out_specs=HBM,
        scratch_shapes=[
            pltpu.VMEM((slabs * MOST, volume, channels), F32),
            pltpu.VMEM((total * volume, channels), BF16),
            pltpu.VMEM((total, EDGE, EDGE * EDGE, channels), F32),
            pltpu.VMEM((2 * total * volume, channels), F32),
            pltpu.VMEM((3, total, EDGE + 2, EDGE * EDGE, channels), BF16),
            pltpu.VMEM((4, 2 * total * volume, channels), F32),
            pltpu.VMEM(fine_input.shape, BF16),
            pltpu.SemaphoreType.DMA((total,)),
        ],
        compiler_params=limit(18),
        name="final",
    )(
        coords,
        links,
        *replies,
        *lines,
        norm_gain.reshape(1, channels),
        norm_bias.reshape(1, channels),
        lift_weight,
        fine,
        folded,
        *pieces,
    )


def solution(mesh):
    in_specs = (
        P(("scene", "slab"), "sub", None, None),
        P(),
        P(),
        P(),
        P(),
        P(("scene", "slab", "sub"), None, None),
        P(("scene", "slab", "sub"), None),
        P(("scene", "slab", "sub"), None),
        P(),
    )
    out_specs = P(("scene", "slab", "sub"), None, None)
    return jax.shard_map(body, mesh=mesh, in_specs=in_specs, out_specs=out_specs, check_vma=False)
```

```python
import functools

import jax
import jax.numpy as jnp
from jax import lax
from jax.experimental import pallas as pl
from jax.experimental.pallas import tpu as pltpu
from jax.sharding import PartitionSpec as P


G = 32
FB = 8
EDGE = FB // 2
MOST = 2
TAIL = 16
SENT = jnp.bfloat16
EPS = 1e-05
F32 = jnp.float32
BF16 = jnp.bfloat16


def pairs(count, odd):
    links = []
    for i in range(odd, count - 1, 2):
        links += [(i, i + 1), (i + 1, i)]
    return links


def xor_links(count, distance):
    return [(i, i ^ distance) for i in range(count)]


def shifted_sum(sums, depth, channels):
    rows = sums.shape[0]
    place = lax.broadcasted_iota(jnp.int32, (rows, channels), 0) % depth
    below = pltpu.roll(sums[:, :channels], 1, 0)
    above = pltpu.roll(sums[:, 2 * channels :], rows - 1, 0)
    return (
        sums[:, channels : 2 * channels]
        + jnp.where(place == 0, 0.0, below)
        + jnp.where(place == depth - 1, 0.0, above)
    )


def convolved(get, weight, outer, depth):
    channels = weight.shape[1]
    taken = jnp.concatenate(
        [
            jnp.concatenate([get(i + a, b) for i in range(outer)], axis=0)
            for a in range(3)
            for b in range(3)
        ],
        axis=1,
    )
    taps = jnp.concatenate(
        [jnp.concatenate([weight[3 * ab], weight[3 * ab + 1]], axis=1) for ab in range(9)], axis=0
    )
    sums = jnp.dot(taken, taps, preferred_element_type=F32)
    zero = jnp.zeros((channels, channels), BF16)
    taken = jnp.concatenate(
        [
            jnp.concatenate([get(i + a, b) for i in range(0, outer, 2)], axis=0)
            for a in range(4)
            for b in range(3)
        ],
        axis=1,
    )
    taps = jnp.concatenate(
        [
            jnp.concatenate(
                [
                    weight[3 * (3 * a + b) + 2] if a < 3 else zero,
                    weight[3 * (3 * a - 3 + b) + 2] if a else zero,
                ],
                axis=1,
            )
            for a in range(4)
            for b in range(3)
        ],
        axis=0,
    )
    above = jnp.dot(taken, taps, preferred_element_type=F32)
    rows = sums.shape[0]
    plane = rows // outer
    above = jnp.concatenate(
        [
            above[i // 2 * plane : (i // 2 + 1) * plane, i % 2 * channels : (i % 2 + 1) * channels]
            for i in range(outer)
        ],
        axis=0,
    )
    place = lax.broadcasted_iota(jnp.int32, (rows, channels), 0) % depth
    return (
        sums[:, channels:]
        + jnp.where(place == 0, 0.0, pltpu.roll(sums[:, :channels], 1, 0))
        + jnp.where(place == depth - 1, 0.0, pltpu.roll(above, rows - 1, 0))
    )


def neighbour(links, n, direction, total):
    target = links[n, direction]
    return lax.rem(jnp.maximum(target, 0), total), target >= 0


def fold_weights(weight, out):
    channels = weight.shape[1]
    taps = (((0,), (1, 2)), ((0, 1), (2,)))
    for p in range(2):
        for q in range(2):
            for a in range(2):
                for b in range(2):
                    sums = []
                    for c in range(3):
                        parts = [
                            weight[9 * i + 3 * j + c].astype(F32)
                            for i in taps[p][a]
                            for j in taps[q][b]
                        ]
                        sums.append(functools.reduce(jnp.add, parts))
                    kinds = [sums[1] + sums[2], sums[0], sums[0] + sums[1], sums[2]]
                    rows = pl.ds((2 * a + b) * channels, channels)
                    for k, kind in enumerate(kinds):
                        out[2 * p + q, rows, pl.ds(k * channels, channels)] = kind.astype(BF16)


def parity(name, length):
    return jnp.where(lax.rem(lax.axis_index(name), 2) == 0, length - 1, 0)


def send_kernel(inp, coords, links, send_a, send_b, row_a, row_b, coords_out, links_out, note, sems):
    dx, dy = inp.shape[:2]
    xa, ya = parity("slab", dx), parity("sub", dy)
    moves = [
        (coords, coords_out),
        (inp.at[xa], send_a.at[pl.ds(0, dy)]),
        (inp.at[dx - 1 - xa], send_b.at[pl.ds(0, dy)]),
        (inp.at[:, ya], row_a),
        (inp.at[:, dy - 1 - ya], row_b),
        (links, links_out),
    ]
    copies = [pltpu.make_async_copy(a, b, sems.at[i]) for i, (a, b) in enumerate(moves)]
    for copy in copies:
        copy.start()
    note[...] = jnp.zeros_like(note)
    copies[0].wait()
    note[pl.ds(0, coords.shape[0]), pl.ds(0, coords.shape[1])] = coords_out[...] + 1
    send_a[dy] = note[...].astype(F32).astype(BF16)
    send_b[dy] = send_a[dy]
    send_b[dy + 1] = jnp.zeros_like(send_a[dy])
    for copy in copies[1:]:
        copy.wait()


def relay_kernel(x_first, _, send_b):
    send_b[send_b.shape[0] - 1] = x_first[x_first.shape[0] - 1]


def inside(xor, slabs):
    slab = lax.axis_index("slab")
    return jnp.logical_or(not xor, jnp.logical_and(slab > 0, slab < slabs - 1))


def line_kernel(slabs, xor, x_first, x_second, row_a, row_b, line_a, line_b):
    dx, dy = row_a.shape[0], x_first.shape[0] - 1
    has = inside(xor, slabs)
    ya = parity("sub", dy)
    for place, row, line in ((ya, row_a, line_a), (dy - 1 - ya, row_b, line_b)):
        line[0] = x_first[place]
        line[pl.ds(1, dx)] = row[...]
        line[dx + 1] = jnp.where(has, x_second[place], jnp.zeros_like(x_second[place]))


def fine_kernel(first, count, role, *refs):
    loads = []
    if role == "load":
        links, fine_from, weight_from, _, inp = refs[:5]
        out, fine, weight, padded, folded, even, odd, sems = refs[5:]
        dx, dy = inp.shape[:2]
        moves = [
            (fine_from, fine),
            (weight_from, weight),
            (inp, padded.at[pl.ds(1, dx), pl.ds(1, dy)]),
        ]
        loads = [pltpu.make_async_copy(a, b, sems.at[i]) for i, (a, b) in enumerate(moves)]
        for load in loads:
            load.start()
        for y in (0, dy + 1):
            padded[:, y] = jnp.zeros((dx + 2,) + padded.shape[2:], BF16)
        loads[0].wait()
    else:
        links, fine, weight, _, out, even, odd = refs
    total, _, channels = fine.shape
    tile = 2 * FB
    lines = FB // 2

    def plane(n, i):
        return fine[n, pl.ds(i * FB * FB, FB * FB), :].reshape(lines, tile, channels)

    zero = jnp.zeros((FB, channels), F32)
    for slot in range(count):
        n = first + slot
        sides = [neighbour(links, n, direction, total) for direction in range(4)]
        for i in range(-1, FB + 1):
            if 0 <= i < FB:
                here = plane(n, i)
                (low, low_on), (high, high_on) = sides[2], sides[3]
                before = fine[low, pl.ds(i * FB * FB + FB * FB - tile, tile), :].astype(F32)
                after = fine[high, pl.ds(i * FB * FB, tile), :].astype(F32)
                before = jnp.where(low_on, before[FB:], 0.0)
                after = jnp.where(high_on, after[:FB], 0.0)
            else:
                other, on = sides[0] if i < 0 else sides[1]
                here = plane(other, FB - 1 if i < 0 else 0)
                here = jnp.where(on, here, jnp.zeros_like(here))
                before = after = zero
            even[slot, i + 1] = here
            wide = here.astype(F32)
            halves = [before]
            for line in range(lines):
                halves += [wide[line, :FB], wide[line, FB:]]
            halves.append(after)
            for line in range(lines + 1):
                odd[slot, i + 1, line] = jnp.concatenate(
                    halves[2 * line : 2 * line + 2], axis=0
                ).astype(BF16)
        if role == "load" and slot == 0:
            loads[1].wait()

        def get(plane_index, b, slot=slot):
            if b == 1:
                part = even[slot, plane_index]
            else:
                part = odd[slot, plane_index, pl.ds(b // 2, lines)]
            return part.reshape(FB * FB, channels)

        out[slot] = convolved(get, weight, FB, FB)
    if role == "load":
        fold_weights(weight, folded)
    for load in loads[2:]:
        load.wait()


def choose(notes, y_cubes):
    rows = [jnp.concatenate([note[k : k + 1] for note in notes], axis=0) for k in range(3)]
    lane = lax.broadcasted_iota(jnp.int32, rows[0].shape, 1)
    slab = lax.axis_index("slab").astype(F32)
    low = (lax.axis_index("sub") * y_cubes).astype(F32)
    blank = rows[0] != slab + 1.0
    hit = jnp.where(blank, 0.0, 1.0)
    upto = hit
    for step in (1, 2, 4, 8, 16, 32, 64):
        upto = upto + jnp.where(lane >= step, pltpu.roll(upto, step, 1), 0.0)
    result = jnp.zeros(rows[0].shape, F32)
    for slot in range(MOST):
        here = hit * jnp.where(upto == slot + 1.0, 1.0, 0.0)
        for k, cube in enumerate((rows[1] - 1.0 - low, rows[2] - 1.0)):
            first = jnp.sum(here * cube, axis=1, keepdims=True) * EDGE
            result = jnp.where(lane == 2 * slot + k, first, result)
    return result.astype(jnp.int32)


def thirds(value):
    parts = []
    for _ in range(3):
        part = value.astype(BF16)
        parts.append(part)
        value = value - part.astype(F32)
    return parts


def whole_of(rows):
    return jnp.sum(rows.astype(F32), axis=0, keepdims=True)


def coarse_kernel(slabs, xor, cells_shape, *refs):
    _, own, far, x_first, x_second, weight, _ = refs[:7]
    padded, conv, stats, picks, sems = refs[7:]
    dx, dy, dz = cells_shape
    sources = slabs
    asked = [own[dy], x_first[dy], far[dy + 1], far[dy]] if xor else [far[s] for s in range(sources)]
    channels = padded.shape[-1]
    rows = pl.ds(1, dy)
    xa = jnp.where(lax.rem(lax.axis_index("slab"), 2) == 0, dx + 1, 0)
    xb = dx + 1 - xa
    has = inside(xor, slabs)
    first = pltpu.make_async_copy(x_first.at[pl.ds(0, dy)], padded.at[xa, rows], sems.at[0])
    first.start()

    @pl.when(has)
    def _():
        second = pltpu.make_async_copy(x_second.at[pl.ds(0, dy)], padded.at[xb, rows], sems.at[1])
        second.start()
        second.wait()

    @pl.when(jnp.logical_not(has))
    def _():
        padded[xb, rows] = jnp.zeros((dy,) + padded.shape[2:], BF16)

    first.wait()
    means, squares = [], []
    for x in range(dx):
        if x % 2 == 0:

            def get(plane_index, b, x=x):
                return padded[x + plane_index, pl.ds(b, dy)].reshape(dy * dz, channels)

            both = convolved(get, weight, 2, dz).reshape(2, dy, dz, channels)
        value = both[x % 2]
        conv[x] = value
        if x == 0:
            picks[...] = choose([note.astype(F32) for note in asked], dy // EDGE)
        inner = value[1 : dy - 1].reshape(-1, 8, channels)
        mean = jnp.sum(jnp.sum(inner, axis=0), axis=0, keepdims=True) / ((dy - 2) * dz)
        off = conv[x, pl.ds(1, dy - 2)].reshape(-1, 8, channels) - mean[None]
        means.append(mean)
        squares.append(jnp.sum(jnp.sum(off * off, axis=0), axis=0, keepdims=True))
    mean, square = merge(means, squares, float((dy - 2) * dz))
    stats[0:1, :] = mean
    stats[1:2, :] = square


def edge_kernel(sources, xor, *refs):
    picks, conv_from, stats, y_first, y_second, weight = refs[:6]
    outs = refs[6:-3]
    conv, rim, cube = refs[-3:]
    dx, dy, dz, channels = conv.shape
    slab = lax.axis_index("slab")
    sub = lax.axis_index("sub")
    xa = jnp.where(lax.rem(slab, 2) == 0, dx + 1, 0)
    xb = dx + 1 - xa
    side = jnp.where(lax.rem(sub, 2) == 0, 1, 0)
    for got, place in ((y_first, side), (y_second, 1 - side)):
        rim[place, xa] = got[0]
        rim[place, pl.ds(1, dx)] = got[pl.ds(1, dx)]
        rim[place, xb] = got[dx + 1]
    edges = []
    for place, row, b in ((0, 0, 0), (1, dy - 1, 2)):
        taken = [rim[place, pl.ds(a, dx)].reshape(dx * dz, channels) for a in range(3)]
        taps = jnp.concatenate(
            [
                jnp.concatenate([weight[9 * a + 3 * b + c] for c in range(3)], axis=1)
                for a in range(3)
            ],
            axis=0,
        )
        sums = jnp.dot(jnp.concatenate(taken, axis=1), taps, preferred_element_type=F32)
        value = conv_from[:, row] + shifted_sum(sums, dz, channels).reshape(dx, dz, channels)
        conv[:, row] = value
        edges.append(value.reshape(-1, 8, channels))
    count = 2 * dx * dz
    mean = sum(jnp.sum(jnp.sum(e, axis=0), axis=0, keepdims=True) for e in edges) / count
    square = sum(
        jnp.sum(jnp.sum((e - mean[None]) ** 2, axis=0), axis=0, keepdims=True) for e in edges
    )
    cells = dx * dy * dz
    apart = mean - stats[0:1, :]
    square = square + stats[1:2, :] + apart * apart * (count * (cells - count) / cells)
    mean = stats[0:1, :] + apart * (count / cells)
    tail = jnp.concatenate(thirds(mean) + thirds(square), axis=0).astype(F32)
    tail = jnp.concatenate([tail, jnp.zeros((TAIL - 6, channels), F32)], axis=0).astype(SENT)
    for s in range(sources):
        out = outs[s] if xor else outs[0].at[s]
        for slot in range(MOST):
            first_y = picks[s, 2 * slot]
            first_z = picks[s, 2 * slot + 1]
            for x in range(EDGE):
                for y in range(EDGE):
                    piece = conv[x, first_y + y, pl.ds(first_z, EDGE), :]
                    cube[pl.ds(slot * EDGE**3 + (x * EDGE + y) * EDGE, EDGE), :] = piece
        out[pl.ds(0, MOST * EDGE**3), :] = (cube[...] - mean).astype(SENT)
        out[pl.ds(MOST * EDGE**3, TAIL), :] = tail


def group_sum(value, size):
    lanes = value.shape[-1]
    place = lax.broadcasted_iota(jnp.int32, value.shape, 1) % size
    total = value
    for step in range(1, size):
        total = total + jnp.where(place >= step, pltpu.roll(value, step, 1), 0.0)
        total = total + jnp.where(place + step < size, pltpu.roll(value, lanes - step, 1), 0.0)
    return total


def merge(means, squares, count):
    mean = sum(means) / len(means)
    square = sum(squares)
    for part in means:
        square = square + count * (part - mean) * (part - mean)
    return mean, square


def final_kernel(cube_lists, stat_lists, cells, xor, *refs):
    coords, links = refs[:2]
    cubes = refs[2 : 2 + cube_lists]
    stats = refs[2 + cube_lists : 2 + cube_lists + stat_lists]
    rest = refs[2 + cube_lists + stat_lists :]
    gain, bias, lift, fine, folded = rest[:5]
    pieces, out_to = rest[5:-9], rest[-9]
    held, acted, lifted, twice, frame, spread, out, sems = rest[-8:]
    total, _, channels = fine.shape
    slab = lax.axis_index("slab")
    volume = EDGE**3
    if not xor:
        for slot in range(MOST):
            for s in range(cubes[0].shape[0]):
                held[MOST * s + slot] = cubes[0][s, pl.ds(slot * volume, volume), :].astype(F32) + whole_of(
                    cubes[0][s, pl.ds(MOST * volume, 3), :]
                )
    size = channels // G
    mean, square = merge(
        [s[0:1, :] for s in stats], [s[1:2, :] for s in stats], float(cells)
    )
    cells = cells * stat_lists
    group_mean = group_sum(mean, size) / size
    off = mean - group_mean
    group_var = group_sum(square + cells * off * off, size) / (cells * size)
    scale = lax.rsqrt(group_var + EPS) * gain[...]

    def act(value, n):
        normed = (value - group_mean) * scale + bias[...]
        rows = pl.ds(pl.multiple_of(n * volume, volume), volume)
        acted[rows, :] = (normed / (1.0 + jnp.exp(-normed))).astype(BF16)

    seen = [[jnp.int32(0)] * MOST for _ in cubes]
    for n in range(total):
        holder = coords[0, n]
        rank = jnp.int32(0)
        for m in range(n):
            rank = rank + (coords[0, m] == holder).astype(jnp.int32)
        if xor:
            source = jnp.bitwise_xor(holder, slab)
            for s in range(len(cubes)):
                for slot in range(MOST):
                    here = jnp.logical_and(source == s, rank == slot)
                    seen[s][slot] = jnp.where(here, n, seen[s][slot])
        else:
            act(held[holder * MOST + rank], n)
    if xor:
        for s, cube in enumerate(cubes):
            base = whole_of(cube[pl.ds(MOST * volume, TAIL), :][0:3])
            for slot in range(MOST):
                act(cube[pl.ds(slot * volume, volume), :].astype(F32) + base, seen[s][slot])
    rounded = jnp.dot(acted[...], lift[...], preferred_element_type=F32).astype(BF16).astype(F32)
    rows = total * volume
    twice[pl.ds(0, rows, stride=2), :] = rounded
    twice[pl.ds(1, rows, stride=2), :] = rounded
    flat = EDGE * EDGE
    lifted[...] = rounded.reshape(total, EDGE, flat, channels)
    place = lax.broadcasted_iota(jnp.int32, (flat, channels), 0)
    for n in range(total):
        sides = [neighbour(links, n, direction, total) for direction in range(4)]
        for i in range(-1, EDGE + 1):
            if 0 <= i < EDGE:
                here = lifted[n, i]
                (low, low_on), (high, high_on) = sides[2], sides[3]
                before = jnp.where(low_on, lifted[low, i], 0.0)
                after = jnp.where(high_on, lifted[high, i], 0.0)
                before = pltpu.roll(before, EDGE, 0)
                after = pltpu.roll(after, flat - EDGE, 0)
            else:
                other, on = sides[0] if i < 0 else sides[1]
                here = jnp.where(on, lifted[other, EDGE - 1 if i < 0 else 0], 0.0)
                before = after = jnp.zeros_like(here)
            frame[0, n, i + 1] = jnp.where(
                place < EDGE, before, pltpu.roll(here, EDGE, 0)
            ).astype(BF16)
            frame[1, n, i + 1] = here.astype(BF16)
            frame[2, n, i + 1] = jnp.where(
                place >= flat - EDGE, after, pltpu.roll(here, flat - EDGE, 0)
            ).astype(BF16)
    whole = [piece.at[n] for piece in pieces for n in range(piece.shape[0])]
    step = total // 2
    band = step * volume
    level = lax.broadcasted_iota(jnp.int32, (band, channels), 0) % EDGE
    copies = []
    for first in range(0, total, step):
        for p in range(2):
            for q in range(2):
                taken = [
                    frame[q + b, pl.ds(first, step), pl.ds(p + a, EDGE)].reshape(band, channels)
                    for a in range(2)
                    for b in range(2)
                ]
                sums = jnp.dot(
                    jnp.concatenate(taken, axis=1), folded[2 * p + q], preferred_element_type=F32
                )
                below = pltpu.roll(sums[:, channels : 2 * channels], 1, 0)
                above = pltpu.roll(sums[:, 3 * channels :], band - 1, 0)
                even = sums[:, :channels] + jnp.where(level == 0, 0.0, below)
                odd = sums[:, 2 * channels : 3 * channels] + jnp.where(
                    level == EDGE - 1, 0.0, above
                )
                start = 2 * first * volume
                spread[2 * p + q, pl.ds(start, band, stride=2), :] = even
                spread[2 * p + q, pl.ds(start + 1, band, stride=2), :] = odd
            for n in range(first, first + step):
                for i in range(p, FB, 2):
                    for j in range(0, FB, 2):
                        cell = pl.ds(((n * EDGE + i // 2) * EDGE + j // 2) * FB, FB)
                        pair = pl.ds((i * FB + j) * FB, 2 * FB)
                        up = twice[cell, :]
                        raised = jnp.concatenate([up, up], axis=0)
                        own = (fine[n, pair, :].astype(F32) + raised).astype(BF16).astype(F32)
                        conv = jnp.concatenate(
                            [spread[2 * p, cell, :], spread[2 * p + 1, cell, :]], axis=0
                        )
                        out[n, pair, :] = (own + whole[n][pair, :] + conv).astype(BF16)
                if p:
                    copies.append(pltpu.make_async_copy(out.at[n], out_to.at[n], sems.at[n]))
                    copies[-1].start()
    for copy in copies:
        copy.wait()


SMEM = pl.BlockSpec(memory_space=pltpu.SMEM)
VMEM = pl.BlockSpec(memory_space=pltpu.VMEM)
HBM = pl.BlockSpec(memory_space=pl.ANY)


def limit(mib):
    return pltpu.CompilerParams(vmem_limit_bytes=mib * 2**20)


def fine_part(links, fine, weight, after, first, count, role, coarse_in=None):
    _, cells, channels = fine.shape
    shapes = [jax.ShapeDtypeStruct((count, cells, channels), F32)]
    specs, sems, inputs = [SMEM, VMEM, VMEM, HBM], [], (links, fine, weight, after)
    if role == "load":
        dx, dy, dz, _ = coarse_in.shape
        extra = [fine.shape, weight.shape, (dx + 2, dy + 2, dz, channels)]
        extra.append((4, 4 * channels, 4 * channels))
        shapes += [jax.ShapeDtypeStruct(shape, BF16) for shape in extra]
        hbm = pl.BlockSpec(memory_space=pltpu.HBM)
        specs = [SMEM, hbm, hbm, HBM, hbm]
        sems = [pltpu.SemaphoreType.DMA((3,))]
        fine, weight, coarse_in = (
            pltpu.with_memory_space_constraint(x, pltpu.HBM) for x in (fine, weight, coarse_in)
        )
        inputs = (links, fine, weight, after, coarse_in)
    return pl.pallas_call(
        functools.partial(fine_kernel, first, count, role),
        out_shape=shapes,
        in_specs=specs,
        out_specs=[VMEM] * len(shapes),
        scratch_shapes=[
            pltpu.VMEM((count, FB + 2, FB // 2, 2 * FB, channels), BF16),
            pltpu.VMEM((count, FB + 2, FB // 2 + 1, 2 * FB, channels), BF16),
        ]
        + sems,
        compiler_params=limit(18),
        cost_estimate=pl.CostEstimate(
            flops=2 * 27 * count * cells * channels * channels,
            bytes_accessed=4 * count * cells * channels,
            transcendentals=0,
        ),
        name="fine_part",
    )(*inputs)


def body(
    coarse_in,
    coarse_weight,
    norm_gain,
    norm_bias,
    lift_weight,
    fine_input,
    block_coords,
    neighbours,
    fine_weight,
):
    dx, dy, dz, channels = coarse_in.shape
    slabs, subs = lax.axis_size("slab"), lax.axis_size("sub")
    total = block_coords.shape[0]
    xor = slabs == 4 and total == MOST * slabs
    coords = block_coords.T
    send_a, send_b, row_a, row_b, coords, links = pl.pallas_call(
        send_kernel,
        out_shape=[
            jax.ShapeDtypeStruct((dy + 1, dz, channels), BF16),
            jax.ShapeDtypeStruct((dy + 2, dz, channels), BF16),
            jax.ShapeDtypeStruct((dx, dz, channels), BF16),
            jax.ShapeDtypeStruct((dx, dz, channels), BF16),
            jax.ShapeDtypeStruct(coords.shape, jnp.int32),
            jax.ShapeDtypeStruct(neighbours.shape, jnp.int32),
        ],
        in_specs=[pl.BlockSpec(memory_space=pltpu.HBM)] * 3,
        out_specs=[VMEM] * 6,
        scratch_shapes=[pltpu.VMEM((dz, channels), jnp.int32), pltpu.SemaphoreType.DMA((6,))],
        compiler_params=limit(4),
        name="send",
    )(*(pltpu.with_memory_space_constraint(x, pltpu.HBM) for x in (coarse_in, coords, neighbours)))
    x_first = lax.ppermute(send_a, "slab", pairs(slabs, 0))
    if xor:
        send_b = pl.pallas_call(
            relay_kernel,
            out_shape=jax.ShapeDtypeStruct(send_b.shape, BF16),
            in_specs=[VMEM] * 2,
            out_specs=VMEM,
            input_output_aliases={1: 0},
            compiler_params=limit(4),
            name="relay",
        )(x_first, send_b)
        far = x_second = lax.ppermute(send_b, "slab", xor_links(slabs, 3))
    else:
        x_second = lax.ppermute(send_b, "slab", pairs(slabs, 1))
        far = lax.all_gather(send_a[dy], "slab", axis=0)
    shares = [0, total * 3 // 8, total * 3 // 4, total]
    pieces = []

    def fill(index, after, waiting, role="plain"):
        begin = shares[index]
        count = shares[index + 1] - begin
        made = fine_part(links, fine, weight, after, begin, count, role, coarse_in)
        made, waiting = lax.optimization_barrier((made, waiting))
        pieces.append(made[0])
        return made[1:], waiting

    fine, weight = fine_input, fine_weight
    made, x_second = fill(0, send_b, x_second, "load")
    if xor:
        far = x_second
    fine, weight, padded, folded = made
    line_a, line_b = pl.pallas_call(
        functools.partial(line_kernel, slabs, xor),
        out_shape=[jax.ShapeDtypeStruct((dx + 2, dz, channels), BF16)] * 2,
        in_specs=[VMEM] * 4,
        out_specs=[VMEM] * 2,
        compiler_params=limit(4),
        name="line",
    )(x_first, x_second, row_a, row_b)
    y_first = lax.ppermute(line_a, "sub", pairs(subs, 0))
    y_second = lax.ppermute(line_b, "sub", pairs(subs, 1))

    padded, conv, stats, picks = pl.pallas_call(
        functools.partial(coarse_kernel, slabs, xor, (dx, dy, dz)),
        out_shape=[
            jax.ShapeDtypeStruct(padded.shape, BF16),
            jax.ShapeDtypeStruct(coarse_in.shape, F32),
            jax.ShapeDtypeStruct((8, channels), F32),
            jax.ShapeDtypeStruct((slabs, channels), jnp.int32),
        ],
        in_specs=[VMEM] * 6 + [HBM],
        out_specs=[VMEM] * 4,
        scratch_shapes=[pltpu.SemaphoreType.DMA((2,))],
        input_output_aliases={0: 0},
        compiler_params=limit(12),
        cost_estimate=pl.CostEstimate(
            flops=2 * 27 * dx * dy * dz * channels * channels,
            bytes_accessed=4 * dx * dy * dz * channels,
            transcendentals=0,
        ),
        name="coarse",
    )(padded, send_a, far, x_first, x_second, coarse_weight, line_a)
    (conv, stats), (y_first, y_second) = lax.optimization_barrier(
        ((conv, stats), (y_first, y_second))
    )
    piece = (MOST * EDGE**3 + TAIL, channels)
    if xor:
        shapes = [jax.ShapeDtypeStruct(piece, SENT)] * slabs
    else:
        shapes = [jax.ShapeDtypeStruct((slabs,) + piece, SENT)]
    results = pl.pallas_call(
        functools.partial(edge_kernel, slabs, xor),
        out_shape=shapes + [jax.ShapeDtypeStruct(conv.shape, F32)],
        in_specs=[SMEM] + [VMEM] * 5,
        out_specs=[VMEM] * (len(shapes) + 1),
        scratch_shapes=[
            pltpu.VMEM((2, dx + 2, dz, channels), BF16),
            pltpu.VMEM((MOST * EDGE**3, channels), F32),
        ],
        input_output_aliases={1: len(shapes)},
        compiler_params=limit(8),
        name="edge",
    )(picks, conv, stats, y_first, y_second, coarse_weight)
    sent = results[:-1]
    cells = dx * dy * dz
    row = MOST * EDGE**3
    if xor:
        replies = [sent[0]]
        for distance in range(1, slabs):
            replies.append(lax.ppermute(sent[distance], "slab", xor_links(slabs, distance)))
        parts = [r[row : row + 6] for r in replies]
    else:
        replies = [lax.all_to_all(sent[0], "slab", split_axis=0, concat_axis=0, tiled=True)]
        parts = [replies[0][s, row : row + 6] for s in range(slabs)]
    _, parts = fill(1, sent[0], parts)
    mean, square = merge([whole_of(p[0:3]) for p in parts], [whole_of(p[3:6]) for p in parts], float(cells))
    cells = cells * slabs
    merged = jnp.concatenate([mean, square])
    if subs == 4:
        lines = [merged]
        for distance in range(1, subs):
            lines.append(lax.ppermute(merged, "sub", xor_links(subs, distance)))
    else:
        lines = list(lax.all_gather(merged, "sub", axis=0))
    _, lines = fill(2, merged, lines)

    volume = EDGE**3
    return pl.pallas_call(
        functools.partial(final_kernel, len(replies), len(lines), cells, xor),
        out_shape=jax.ShapeDtypeStruct(fine_input.shape, BF16),
        in_specs=[SMEM] * 2 + [VMEM] * (len(replies) + len(lines) + 5 + len(pieces)),
        out_specs=HBM,
        scratch_shapes=[
            pltpu.VMEM((slabs * MOST, volume, channels), F32),
            pltpu.VMEM((total * volume, channels), BF16),
            pltpu.VMEM((total, EDGE, EDGE * EDGE, channels), F32),
            pltpu.VMEM((2 * total * volume, channels), F32),
            pltpu.VMEM((3, total, EDGE + 2, EDGE * EDGE, channels), BF16),
            pltpu.VMEM((4, 2 * total * volume, channels), F32),
            pltpu.VMEM(fine_input.shape, BF16),
            pltpu.SemaphoreType.DMA((total,)),
        ],
        compiler_params=limit(18),
        name="final",
    )(
        coords,
        links,
        *replies,
        *lines,
        norm_gain.reshape(1, channels),
        norm_bias.reshape(1, channels),
        lift_weight,
        fine,
        folded,
        *pieces,
    )


def solution(mesh):
    in_specs = (
        P(("scene", "slab"), "sub", None, None),
        P(),
        P(),
        P(),
        P(),
        P(("scene", "slab", "sub"), None, None),
        P(("scene", "slab", "sub"), None),
        P(("scene", "slab", "sub"), None),
        P(),
    )
    out_specs = P(("scene", "slab", "sub"), None, None)
    return jax.shard_map(body, mesh=mesh, in_specs=in_specs, out_specs=out_specs, check_vma=False)
```
